128 devices in a mesh: slab: 16 (over y, x), gore: 8 (over z, core).
Axes of the slice: x: 4, y: 4, z: 4, core: 2. Of those that a mesh axis runs over, the one named last changes fastest.
Arguments:
- fluid_velocity: float32 [3, 128, 256, 1024], P(None, 'slab', 'gore'), may hold values from -6 to 6
- viscosity: float32 [128, 256, 1024], P('slab', 'gore'), may hold values from 0.03 to 0.16
- pressure_jump: float32 [1024, 1024], P('slab', 'gore'), may hold values from -6 to 6
- normals: float32 [3, 1024, 1024], P(None, 'slab', 'gore'), may hold values from -6 to 6
- canopy_position: float32 [3, 1024, 1024], P(None, 'slab', 'gore'), may hold values from -6 to 6
- tension: float32 [4, 1024, 1024], P(None, 'slab', 'gore'), may hold values from 0.5 to 4
- slot_cut: int32 [1024], replicated, may hold values 0 or 1
- couple_dest: int32 [8, 1024, 2], P('gore', 'slab'), may hold values from 0 to 127, all different within a row; in each aligned block of 64 rows (0 to 63, 64 to 127, ..., all dimensions but the last counted through in order) at most 2 rows name the same one
- couple_block: int32 [8, 1024, 2], P('gore', 'slab'), may hold values from 0 to 2047
- contact_owner: int32 [8, 128, 1], P('gore', 'slab'), may hold values from 0 to 7; in each aligned block of 8 rows (0 to 7, 8 to 15, ..., all dimensions but the last counted through in order) at most 2 rows name the same one
- contact_row: int32 [8, 128], P('gore', 'slab'), may hold values from 0 to 63
Outputs:
- fluid_out: float32 [3, 128, 256, 1024], P(None, 'slab', 'gore')
- canopy_out: float32 [3, 1024, 1024], P(None, 'slab', 'gore')
- contact_force: float32 [16, 8, 16, 3, 128], P('slab', 'gore')
The draws below stay inside these ranges and needn't reach their ends.
Inputs may be any that keep to these rules, and one draw needn't show every extreme that they name: `couple_dest`: each row names 2 different devices; among the rows of one device no device is named more than 2 times, and some device's rows name one exactly 2 times. `contact_owner`: among the 8 entries of one device no owner is named more than 2 times, and some device names one exactly 2 times.
All inputs are finite; a program needn't handle non-finite values.
Results may differ from the reference program's by a relative error of at most 0.0003.
Values sent between devices are 32-bit elements; how exact they have to be, the bound alone decides.
A program may use at most 128 MiB of HBM per device.

```python
import math
import jax
import jax.numpy as jnp
import numpy as np
from jax import lax

NX = 1024
CZ = 8
CY = 32
C_DEV = 128
R_DEV = 64
TOP = 2
STEPS = 3
SWEEPS = 8
LIST_DEV = 8
SLABS = 16
GORES = 8
NZ = 128
NY = 256
ROWS = 1024
COLS = 1024
NBLK = 2048
CAP = 2
CAP_C = 2
OWNER_SLOTS = 16
DEVICES = 128


def place_ends(array, stream_key, least, high):
    longest = array.shape.index(max(array.shape))
    spots = []
    for shift in (0, 1):
        where = [jax.random.randint(jax.random.fold_in(stream_key, axis), (), 0, length) for axis, length in enumerate(array.shape)]
        where[longest] = (where[longest] + shift) % array.shape[longest]
        spots.append(tuple(where))
    return array.at[spots[0]].set(least).at[spots[1]].set(high)


def block_scale(own_key, shape, split, smallest, top_value):
    def one(axis_at, blocks):
        steps = jax.random.uniform(jax.random.fold_in(jax.random.fold_in(own_key, 6), axis_at), (blocks,), jnp.float32, smallest / len(split), top_value / len(split))
        return jnp.repeat(jnp.exp(steps), shape[axis_at] // blocks).reshape((-1,) + (1,) * (len(shape) - axis_at - 1))

    level = one(*split[0])
    for cut in split[1:]:
        level = level * one(*cut)
    return level


def routed_block(own_key, own, number, rows, number_of, top, most, slope):
    order = jax.random.permutation(own_key, number_of)
    crowded, ordinary = load_shares(number_of, rows * top, most, slope, True), load_shares(number_of, rows * top, most, slope, False)
    places = jnp.arange(number_of)

    def named(tallies, offset_by):
        used = int((tallies > 0).sum())
        fixed = max(1, used // 4)
        passed = fixed + (places - fixed + offset_by * (used - fixed)) % max(1, number_of - fixed)
        return jnp.zeros((number_of,), jnp.int32).at[order[jnp.where(places < fixed, places, passed)]].set(jnp.asarray(tallies, jnp.int32))

    tallies = jnp.where(number % 4 == 0, named(crowded, number // 4), named(ordinary, number - number // 4 - 1))
    mixed = jax.random.permutation(jax.random.fold_in(own, 3), number_of)
    giver, receiver = mixed[0:number_of // 2 * 2:2], mixed[1:number_of // 2 * 2:2]
    slack = jnp.minimum(tallies[giver] - 1, most - tallies[receiver]) // 2
    slack = jnp.where((giver == order[0]) | (receiver == order[0]) | (tallies[receiver] == 0), 0, jnp.maximum(slack, 0))
    passed = jax.random.randint(jax.random.fold_in(own, 4), (number_of // 2,), 0, 1 << 20) % (slack + 1)
    tallies = tallies.at[giver].add(-passed).at[receiver].add(passed)
    items = jnp.searchsorted(jnp.cumsum(tallies), jnp.arange(rows * top), side="right").astype(jnp.int32)
    listing = items.reshape(top, rows).T
    listing = listing[jax.random.permutation(jax.random.fold_in(own, 1), rows)]
    offset_by = jax.random.randint(jax.random.fold_in(own, 2), (rows, 1), 0, top)
    return jnp.take_along_axis(listing, (jnp.arange(top)[None, :] + offset_by) % top, axis=1)


def load_shares(count, total, reach, lean, full):
    portions = [(1 << 20) // math.isqrt(rank ** lean) + 1 for rank in range(1, count + 1)]
    largest = reach if full else min(reach, max(-(-total // count), total * portions[0] // sum(portions)))
    least = 1 if total - largest >= count - 1 else 0
    holding, spare = [largest] + [least] * (count - 1), total - largest - least * (count - 1)
    while spare > 0:
        free = [i for i in range(1, count) if holding[i] < largest] or [i for i in range(1, count) if holding[i] < reach]
        mass, remaining = sum([portions[i] for i in free]), spare
        for i in free:
            more = min(reach - holding[i], max(1, remaining * portions[i] // mass), spare)
            holding[i] = holding[i] + more
            spare = spare - more
    return np.array(holding)


def noise(key, extent, width, most, shards=(), kind=jnp.bfloat16):
    level = block_scale(key, extent, shards, -0.22, 0.18) if shards else 1.0
    entries = jax.random.normal(key, extent, jnp.float32) * width * level
    return jnp.minimum(jnp.maximum(entries, -most), most).astype(kind)


def setup_inputs(seed: int = 0) -> dict:
    key_of = jax.random.split(jax.random.key(seed), 12)
    fluid_velocity = noise(key_of[0], (3, NZ, NY, NX), 1.0, 6.0, ((1, 16), (2, 8)), jnp.float32)
    viscosity = jnp.clip(jnp.exp(math.log(0.16) - 1.6739764 * jax.random.uniform(key_of[1], (NZ, NY, NX), jnp.float32) ** block_scale(key_of[1], (NZ, NY, NX), ((0, 16), (1, 8)), -0.2, 0.2)), 0.03, 0.16)
    pressure_jump = noise(key_of[2], (ROWS, COLS), 1.0, 6.0, ((0, 16), (1, 8)), jnp.float32)
    normals = noise(key_of[3], (3, ROWS, COLS), 1.0, 6.0, ((1, 16), (2, 8)), jnp.float32)
    canopy_position = noise(key_of[4], (3, ROWS, COLS), 1.0, 6.0, ((1, 16), (2, 8)), jnp.float32)
    tension = jnp.clip(jnp.exp(math.log(4.0) - 2.0794415 * jax.random.uniform(key_of[5], (4, ROWS, COLS), jnp.float32) ** block_scale(key_of[5], (4, ROWS, COLS), ((1, 16), (2, 8)), -0.2, 0.2)), 0.5, 4.0)
    slot_cut = place_ends((jax.random.randint(key_of[6], (ROWS,), 0, 6) < 1).astype(jnp.int32), jax.random.fold_in(key_of[6], 1), 0, 1)
    couple_dest_keys = jax.random.split(jax.random.fold_in(key_of[7], 1), GORES * ROWS // R_DEV)
    couple_dest_turns = jax.random.permutation(jax.random.fold_in(key_of[7], 3), GORES * ROWS // R_DEV)
    couple_dest = jax.vmap(lambda own, number: routed_block(jax.random.fold_in(key_of[7], 2), own, number, R_DEV, DEVICES, TOP, CAP, 2))(couple_dest_keys, couple_dest_turns).reshape((GORES, ROWS, TOP))
    couple_block = place_ends(jax.random.randint(key_of[8], (GORES, ROWS, TOP), 0, NBLK), jax.random.fold_in(key_of[8], 1), 0, NBLK - 1).astype(jnp.int32)
    contact_owner_keys = jax.random.split(jax.random.fold_in(key_of[9], 1), GORES * (SLABS * LIST_DEV) // LIST_DEV)
    contact_owner_turns = jax.random.permutation(jax.random.fold_in(key_of[9], 3), GORES * (SLABS * LIST_DEV) // LIST_DEV)
    contact_owner = jax.vmap(lambda own, number: routed_block(jax.random.fold_in(key_of[9], 2), own, number, LIST_DEV, GORES, 1, CAP_C, 2))(contact_owner_keys, contact_owner_turns).reshape((GORES, SLABS * LIST_DEV, 1))
    contact_row = place_ends(jax.random.randint(key_of[10], (GORES, SLABS * LIST_DEV), 0, R_DEV), jax.random.fold_in(key_of[10], 1), 0, R_DEV - 1).astype(jnp.int32)
    return {"fluid_velocity": fluid_velocity, "viscosity": viscosity, "pressure_jump": pressure_jump, "normals": normals, "canopy_position": canopy_position, "tension": tension, "slot_cut": slot_cut, "couple_dest": couple_dest, "couple_block": couple_block, "contact_owner": contact_owner, "contact_row": contact_row}


FORCE_SCALE = 0.5
CONTACT_GAIN = 0.1
CONTACT_REACH = 1.0
SOFTEN = 0.01

def pair_force(row_points, row_source, col_points, col_source, col_live):
    differ = row_points[:, :, None] - col_points[:, None, :]
    distance = jnp.sqrt(lax.optimization_barrier(jnp.sum(differ * differ, axis=0)) + SOFTEN)
    spacing = jnp.maximum(CONTACT_REACH - distance, 0.0)
    weight = CONTACT_GAIN * spacing * spacing / distance
    weight = weight * (row_source[:, None] != col_source[None, :]).astype(jnp.float32) * col_live[None, :]
    return lax.optimization_barrier(jnp.sum(differ * weight[None], axis=2))

def set_force(points, source, live):
    total_points = points.shape[1]
    block_rows = math.gcd(total_points, 512)
    blocks_count = total_points // block_rows

    def one_block(number):
        begin = number * block_rows
        row_points = lax.dynamic_slice_in_dim(points, begin, block_rows, 1)
        row_source = lax.dynamic_slice_in_dim(source, begin, block_rows, 0)
        row_live = lax.dynamic_slice_in_dim(live, begin, block_rows, 0)
        return pair_force(row_points, row_source, points, source, live) * row_live[None, :]
    pieces = lax.map(one_block, jnp.arange(blocks_count, dtype=jnp.int32))
    return jnp.moveaxis(pieces, 0, 1).reshape(3, total_points)

def diffuse_one(component, viscosity):
    padded = jnp.pad(component, 1)
    center = padded[1:-1, 1:-1, 1:-1]
    beside = padded[2:, 1:-1, 1:-1] + padded[:-2, 1:-1, 1:-1]
    beside = beside + padded[1:-1, 2:, 1:-1] + padded[1:-1, :-2, 1:-1]
    beside = beside + padded[1:-1, 1:-1, 2:] + padded[1:-1, 1:-1, :-2]
    return center + viscosity * (beside - 6.0 * center)

def reference(fluid_velocity, viscosity, pressure_jump, normals, canopy_position, tension, slot_cut, couple_dest, couple_block, contact_owner, contact_row):
    per_line = NX // C_DEV
    surface = pressure_jump[None] * normals
    surface = surface.reshape(3, ROWS, GORES, C_DEV).transpose(0, 2, 1, 3) * (1.0 / TOP)
    tiles = jnp.broadcast_to(surface[:, :, :, None, :], (3, GORES, ROWS, TOP, C_DEV)).reshape(3, GORES * ROWS * TOP, C_DEV)
    destination = couple_dest.reshape(-1)
    fluid_line = couple_block.reshape(-1)
    z_plane = destination // GORES * CZ + fluid_line // (CY * per_line)
    y_row = destination % GORES * CY + fluid_line // per_line % CY
    target = ((z_plane * NY + y_row) * per_line + fluid_line % per_line).astype(jnp.int32)
    jump_force = jnp.zeros((3, NZ * NY * per_line, C_DEV), jnp.float32).at[:, target, :].add(tiles)
    field = fluid_velocity + FORCE_SCALE * jump_force.reshape(3, NZ, NY, NX)
    for substep in range(STEPS):
        field = lax.map(lambda component: diffuse_one(component, viscosity), field)
    fluid_out = field
    sampled = field.reshape(3, NZ * NY * per_line, C_DEV)[:, target, :].reshape(3, GORES, ROWS, TOP, C_DEV)
    node_velocity = (lax.optimization_barrier(jnp.sum(sampled, axis=3)) * (1.0 / TOP)).transpose(0, 2, 1, 3).reshape(3, ROWS, COLS)
    keep_down = jnp.concatenate([1 - slot_cut[:-1], jnp.zeros((1,), jnp.int32)]).astype(jnp.float32)
    keep_up = jnp.concatenate([jnp.zeros((1,), jnp.float32), keep_down[:-1]])
    w_up = tension[0] * keep_up[:, None]
    w_down = tension[1] * keep_down[:, None]
    w_left = tension[2]
    w_right = tension[3]
    denominator = 1.0 + w_up + w_down + w_left + w_right
    right_side = canopy_position + node_velocity
    current = canopy_position
    for sweep_number in range(SWEEPS):
        above = jnp.roll(current, 1, axis=1)
        below = jnp.roll(current, -1, axis=1)
        before = jnp.roll(current, 1, axis=2)
        after = jnp.roll(current, -1, axis=2)
        current = (right_side + w_up * above + w_down * below + w_left * before + w_right * after) / denominator
    canopy_out = current
    owners = contact_owner[:, :, 0].reshape(GORES, SLABS, LIST_DEV)
    picked_rows = contact_row.reshape(GORES, SLABS, LIST_DEV)
    onehot = (owners[..., None] == jnp.arange(GORES, dtype=jnp.int32)).astype(jnp.int32)
    earlier = jnp.cumsum(onehot, axis=2) - onehot
    ranking = lax.optimization_barrier(jnp.sum(earlier * onehot, axis=3))
    gore_ids = jnp.broadcast_to(jnp.arange(GORES, dtype=jnp.int32)[:, None, None], owners.shape)
    slab_ids = jnp.broadcast_to(jnp.arange(SLABS, dtype=jnp.int32)[None, :, None], owners.shape)
    global_rows = slab_ids * R_DEV + picked_rows
    chosen = canopy_out.reshape(3, ROWS, GORES, C_DEV)[:, global_rows, gore_ids, :]
    slot_ids = gore_ids * CAP_C + ranking
    sets = jnp.zeros((SLABS, GORES, OWNER_SLOTS, 3, C_DEV), jnp.float32).at[slab_ids, owners, slot_ids].set(jnp.moveaxis(chosen, 0, 3))
    filled = jnp.zeros((SLABS, GORES, OWNER_SLOTS), jnp.float32).at[slab_ids, owners, slot_ids].set(1.0)
    source = jnp.repeat(jnp.arange(OWNER_SLOTS, dtype=jnp.int32) // CAP_C, C_DEV)

    def one_set(number):
        slab_at = number // GORES
        owner_at = number % GORES
        points = jnp.moveaxis(sets[slab_at, owner_at], 0, 1).reshape(3, OWNER_SLOTS * C_DEV)
        live = jnp.repeat(filled[slab_at, owner_at], C_DEV)
        forces = set_force(points, source, live)
        return jnp.moveaxis(forces.reshape(3, OWNER_SLOTS, C_DEV), 0, 1)
    all_forces = lax.map(one_set, jnp.arange(SLABS * GORES, dtype=jnp.int32))
    contact_force = all_forces.reshape(SLABS, GORES, OWNER_SLOTS, 3, C_DEV)
    return (fluid_out, canopy_out, contact_force)
```

```python
import functools

import jax
import jax.numpy as jnp
from jax import lax
from jax.experimental import pallas as pl
from jax.experimental.pallas import tpu as pltpu
from jax.sharding import PartitionSpec as P

STEPS = 3
SWEEPS = 8
HALO = 8
LANES = 128
GAIN = 0.1
REACH = 1.0
SOFTEN = 0.01
FAR = 1.0e15
MESH = pl.DeviceIdType.MESH
F32 = jnp.float32
BF16 = jnp.bfloat16


def iota(shape, dim):
    return lax.broadcasted_iota(jnp.int32, shape, dim)


def dot(a, b):
    return lax.dot_general(a, b, (((1,), (0,)), ((), ())), preferred_element_type=F32)


def exact_dot(a, b):
    return lax.dot_general(
        a, b, (((1,), (0,)), ((), ())),
        precision=lax.Precision.HIGHEST, preferred_element_type=F32,
    )


def split(x):
    hi = x.astype(BF16)
    return hi, (x - hi.astype(F32)).astype(BF16)


def to_column(row):
    n = row.shape[1]
    same = iota((n, n), 0) == iota((n, n), 1)
    return jnp.sum(jnp.where(same, jnp.broadcast_to(row, (n, n)), 0.0), axis=1, keepdims=True)


def main_kernel(
    slabs, gores,
    fluid_hbm, visc_hbm, jump, normals, canopy, tension, cut, dest, block, owner, picked,
    fluid_out, canopy_out, sets_out,
    v, vis, yh, ys, outbox, inbox, ansbox, retbox, hot_t, hot,
    sc, sl, sr, dc, dl, dr, ext, inv, csend, crecv,
    load_sem, store_sem, zs_sem, zr_sem, ysend_sem, yr_sem, a2a_sem, mem_s, mem_r, con_sem,
):
    s = lax.axis_index("slab")
    g = lax.axis_index("gore")
    me = s * gores + g
    devices = slabs * gores
    cz, cy, nx = vis.shape
    zy = cz * cy
    nbx = nx // LANES
    rows = jump.shape[0]

    def device(t):
        return (lax.div(t, gores), lax.rem(t, gores))

    def rows_of(t, count):
        return pl.ds(pl.multiple_of(t * 8, 8), count)

    loads = [
        pltpu.make_async_copy(fluid_hbm.at[c], v.at[0, c, pl.ds(1, cz)], load_sem.at[c])
        for c in range(3)
    ]
    loads.append(pltpu.make_async_copy(visc_hbm, vis, load_sem.at[3]))
    for copy in loads:
        copy.start()
    barrier = pltpu.get_barrier_semaphore()

    def greet(i, carry):
        t = lax.rem(me + i, devices)
        pl.semaphore_signal(barrier, inc=1, device_id=device(t), device_id_type=MESH)
        return carry

    lax.fori_loop(1, devices, greet, 0)

    zero_plane = jnp.zeros((cy, nx), F32)
    zero_edge = jnp.zeros((cz, nx), F32)

    @pl.when(s == 0)
    def _():
        for step in range(STEPS):
            for c in range(3):
                v[step, c, 0] = zero_plane

    @pl.when(s == slabs - 1)
    def _():
        for step in range(STEPS):
            for c in range(3):
                v[step, c, cz + 1] = zero_plane

    @pl.when(g == 0)
    def _():
        for step in range(STEPS):
            for c in range(3):
                yh[step, 0, c] = zero_edge

    @pl.when(g == gores - 1)
    def _():
        for step in range(STEPS):
            for c in range(3):
                yh[step, 1, c] = zero_edge

    dest_row = jnp.concatenate([dest[0:1, :], dest[1:2, :]], axis=1).astype(F32)
    line_row = jnp.concatenate([block[0:1, :], block[1:2, :]], axis=1).astype(F32)
    entries = 2 * rows
    dest_col = to_column(dest_row)
    line_col = to_column(line_row) + 1.0
    by_dev = (iota((devices, entries), 0).astype(F32) == dest_row).astype(F32)
    by_entry = (iota((entries, devices), 1).astype(F32) == dest_col).astype(F32)
    row_a = lax.rem(iota((entries, entries), 0), rows)
    row_b = lax.rem(iota((entries, entries), 1), rows)
    rank_dev = dot(by_dev.astype(BF16), (row_a < row_b).astype(BF16))
    rank_entry = dot((row_b < row_a).astype(BF16), by_entry.astype(BF16))
    surface = [jump[...] * normals[c] * 0.25 for c in range(3)]
    columns = [jnp.concatenate([t, t], axis=0) for t in surface]
    columns.append(jnp.broadcast_to(line_col, (entries, LANES)))
    table = jnp.concatenate(columns, axis=1)
    lines = []
    for slot in range(2):
        pick = jnp.where(rank_dev == float(slot), by_dev, 0.0)
        placed = exact_dot(pick, table)
        for c in range(3):
            outbox[pl.ds(3 * slot + c, devices, stride=8), :] = placed[:, c * LANES:(c + 1) * LANES]
        lines.append(placed[:, 3 * LANES:])
    outbox[pl.ds(6, devices, stride=8), :] = jnp.where(
        iota((devices, LANES), 1) < LANES // 2, lines[0], lines[1]
    )
    back_pick = jnp.concatenate(
        [jnp.where(rank_entry == float(slot), by_entry, 0.0) for slot in range(2)], axis=1
    ).astype(BF16)

    first = s * rows
    cut_f = cut[...].astype(F32)
    cut_rows, cut_width = cut.shape
    node = first + iota((rows, cut_width), 0)
    lane = iota((rows, cut_width), 1)
    down = jnp.zeros((rows, cut_width), F32)
    up = jnp.zeros((rows, cut_width), F32)
    total_rows = slabs * rows
    for q in range(cut_rows):
        index = q * cut_width + lane
        keep = jnp.broadcast_to(1.0 - cut_f[q:q + 1, :], (rows, cut_width))
        down += jnp.where((index == node) & (index < total_rows - 1), keep, 0.0)
        up += jnp.where(index == node - 1, keep, 0.0)
    keep_down = jnp.sum(down, axis=1, keepdims=True)
    keep_up = jnp.sum(up, axis=1, keepdims=True)
    w_up = tension[0] * keep_up
    w_down = tension[1] * keep_down
    w_left = tension[2]
    w_right = tension[3]
    scale = 1.0 / (1.0 + w_up + w_down + w_left + w_right)
    inv[...] = scale
    own = pl.ds(HALO, rows)
    for i, w in enumerate((w_up, w_down, w_left, w_right)):
        sc[i, own, :] = w * scale
    for c in range(3):
        sc[4 + c, own, :] = canopy[c]

    pl.semaphore_wait(barrier, devices - 1)
    inbox[rows_of(me, 8), :] = outbox[rows_of(me, 8), :]

    def send_all(source, target, count, sem):
        def one(i, carry):
            t = lax.rem(me + i, devices)
            pltpu.make_async_remote_copy(
                source.at[rows_of(t, count)], target.at[rows_of(me, count)],
                a2a_sem.at[sem], a2a_sem.at[sem + 1],
                device_id=device(t), device_id_type=MESH,
            ).start()
            return carry

        lax.fori_loop(1, devices, one, 0)

    def wait_all(buffer, count, sem):
        part = buffer.at[pl.ds(0, (devices - 1) * count)]
        pltpu.make_async_copy(part, part, a2a_sem.at[sem]).wait()

    send_all(outbox, inbox, 7, 0)
    wait_all(inbox, 7, 1)

    def z_copies(step, c):
        up_copy = pltpu.make_async_remote_copy(
            v.at[step, c, cz], v.at[step, c, 0], zs_sem.at[step, 0, c], zr_sem.at[step, 0, c],
            device_id=(lax.rem(s + 1, slabs), g), device_id_type=MESH,
        )
        down_copy = pltpu.make_async_remote_copy(
            v.at[step, c, 1], v.at[step, c, cz + 1], zs_sem.at[step, 1, c], zr_sem.at[step, 1, c],
            device_id=(lax.rem(s + slabs - 1, slabs), g), device_id_type=MESH,
        )
        return up_copy, down_copy

    def y_copies(step, c):
        up_copy = pltpu.make_async_remote_copy(
            ys.at[step, 0, c], yh.at[step, 0, c], ysend_sem.at[step, 0, c], yr_sem.at[step, 0, c],
            device_id=(s, lax.rem(g + 1, gores)), device_id_type=MESH,
        )
        down_copy = pltpu.make_async_remote_copy(
            ys.at[step, 1, c], yh.at[step, 1, c], ysend_sem.at[step, 1, c], yr_sem.at[step, 1, c],
            device_id=(s, lax.rem(g + gores - 1, gores)), device_id_type=MESH,
        )
        return up_copy, down_copy

    def start_pair(pair, at, length):
        @pl.when(at < length - 1)
        def _():
            pair[0].start()

        @pl.when(at > 0)
        def _():
            pair[1].start()

    def recv_pair(pair, at, length):
        @pl.when(at > 0)
        def _():
            pair[0].wait_recv()

        @pl.when(at < length - 1)
        def _():
            pair[1].wait_recv()

    def sent_pair(pair, at, length):
        @pl.when(at < length - 1)
        def _():
            pair[0].wait_send()

        @pl.when(at > 0)
        def _():
            pair[1].wait_send()

    meta = inbox[pl.ds(6, devices, stride=8), :]
    meta_t = meta.T
    line_t = jnp.concatenate(
        [meta_t[0:1, :], meta_t[LANES // 2:LANES // 2 + 1, :]], axis=1
    )
    parts = []
    for c in range(3):
        tiles = jnp.concatenate(
            [inbox[pl.ds(3 * slot + c, devices, stride=8), :] for slot in range(2)], axis=0
        )
        parts.append(split(tiles))
    first_line = (iota((zy, 2 * devices), 0) * nbx + 1).astype(F32)
    for c in range(3):
        loads[c].wait()
        for x in range(nbx):
            if c == 0:
                hot_t[x] = jnp.where(line_t == first_line + float(x), 1.0, 0.0).astype(BF16)
            matrix = hot_t[x]
            added = dot(matrix, parts[c][0]) + dot(matrix, parts[c][1])
            cols = pl.ds(x * LANES, LANES)
            here = v[0, c, pl.ds(1, cz), :, cols]
            v[0, c, pl.ds(1, cz), :, cols] = here + added.reshape(cz, cy, LANES)
        start_pair(z_copies(0, c), s, slabs)
        for z in range(cz):
            ys[0, 0, c, z:z + 1, :] = v[0, c, z + 1, cy - 1:cy, :]
            ys[0, 1, c, z:z + 1, :] = v[0, c, z + 1, 0:1, :]
        start_pair(y_copies(0, c), g, gores)
    loads[3].wait()

    def neighbours(mid, left, right, base):
        below, above = lax.rem(s + 1, slabs), lax.rem(s + slabs - 1, slabs)
        after, before = lax.rem(g + 1, gores), lax.rem(g + gores - 1, gores)
        whole = pl.ds(HALO, rows)
        head = pl.ds(HALO, HALO)
        tail = pl.ds(rows, HALO)
        over = pl.ds(0, HALO)
        under = pl.ds(rows + HALO, HALO)
        plan = (
            (whole, left, whole, (s, after)),
            (whole, right, whole, (s, before)),
            (tail, mid, over, (below, g)),
            (head, mid, under, (above, g)),
            (tail, left, over, (below, after)),
            (tail, right, over, (below, before)),
            (head, left, under, (above, after)),
            (head, right, under, (above, before)),
        )
        return [
            pltpu.make_async_remote_copy(
                mid.at[:, src], to.at[:, dst], mem_s.at[base + i], mem_r.at[base + i],
                device_id=where, device_id_type=MESH,
            )
            for i, (src, to, dst, where) in enumerate(plan)
        ]

    static_halos = neighbours(sc, sl, sr, 0)
    for copy in static_halos:
        copy.start()

    at_line = (iota((devices, zy), 1) * nbx + 1).astype(F32)
    for slot in range(2):
        named = jnp.broadcast_to(
            meta[:, slot * (LANES // 2):slot * (LANES // 2) + 1], (devices, zy)
        )
        for x in range(nbx):
            hot[x, slot * devices:(slot + 1) * devices, :] = jnp.where(
                named == at_line + float(x), 1.0, 0.0
            ).astype(BF16)

    sub = iota((8, nx), 0)
    lan = iota((8, nx), 1)

    def plane(step, c, z, stage):
        blocks = cy // 8
        center = v[step, c, z + 1, pl.ds(0, 8), :]
        up_roll = jnp.broadcast_to(yh[step, 0, c, pl.ds(z, 1), :], (8, nx))
        down_roll = pltpu.roll(center, 7, 0)
        for yb in range(blocks):
            at = pl.ds(8 * yb, 8)
            rolled = pltpu.roll(center, 1, 0)
            upper = jnp.where(sub == 0, up_roll, rolled)
            if yb + 1 < blocks:
                following = v[step, c, z + 1, pl.ds(8 * yb + 8, 8), :]
                next_roll = pltpu.roll(following, 7, 0)
            else:
                following = None
                next_roll = jnp.broadcast_to(yh[step, 1, c, pl.ds(z, 1), :], (8, nx))
            lower = jnp.where(sub == 7, next_roll, down_roll)
            total = v[step, c, z, at, :] + v[step, c, z + 2, at, :]
            total = total + upper + lower
            total = total + jnp.where(lan == 0, 0.0, pltpu.roll(center, 1, 1))
            total = total + jnp.where(lan == nx - 1, 0.0, pltpu.roll(center, nx - 1, 1))
            new = center + vis[z, at, :] * (total - 6.0 * center)
            v[step + 1, c, z + 1, at, :] = new
            if stage and yb == 0:
                ys[step + 1, 1, c, pl.ds(z, 1), :] = new[0:1, :]
            if stage and yb == blocks - 1:
                ys[step + 1, 0, c, pl.ds(z, 1), :] = new[7:8, :]
            center, up_roll, down_roll = following, rolled, next_roll

    def substep(step, c, stage):
        recv_pair(z_copies(step, c), s, slabs)
        recv_pair(y_copies(step, c), g, gores)
        plane(step, c, 0, stage)
        plane(step, c, cz - 1, stage)
        if stage:
            start_pair(z_copies(step + 1, c), s, slabs)

        def inner(z, carry):
            plane(step, c, z, stage)
            return carry

        lax.fori_loop(1, cz - 1, inner, 0)
        if stage:
            start_pair(y_copies(step + 1, c), g, gores)

    def early(i, carry):
        substep(lax.div(i, 3), lax.rem(i, 3), True)
        return carry

    lax.fori_loop(0, 3 * (STEPS - 1), early, 0)

    def last(c, carry):
        substep(STEPS - 1, c, False)
        pltpu.make_async_copy(
            v.at[STEPS, c, pl.ds(1, cz)], fluid_out.at[c], store_sem.at[c]
        ).start()
        sampled = jnp.zeros((2 * devices, LANES), F32)
        for x in range(nbx):
            cell = v[STEPS, c, pl.ds(1, cz), :, pl.ds(x * LANES, LANES)].reshape(zy, LANES)
            hi, lo = split(cell)
            sampled = sampled + dot(hot[x], hi) + dot(hot[x], lo)
        for slot in range(2):
            ansbox[pl.ds(3 * slot + c, devices, stride=8), :] = (
                sampled[slot * devices:(slot + 1) * devices]
            )
        return carry

    lax.fori_loop(0, 3, last, 0)

    retbox[rows_of(me, 8), :] = ansbox[rows_of(me, 8), :]
    send_all(ansbox, retbox, 6, 2)
    wait_all(retbox, 6, 3)
    for c in range(3):
        hi, lo = split(
            jnp.concatenate(
                [retbox[pl.ds(3 * slot + c, devices, stride=8), :] for slot in range(2)], axis=0
            )
        )
        taken = dot(back_pick, hi) + dot(back_pick, lo)
        node_velocity = (taken[:rows] + taken[rows:]) * 0.5
        dc[c, own, :] = (canopy[c] + node_velocity) * inv[...]

    moving_halos = neighbours(dc, dl, dr, 8)
    for copy in moving_halos:
        copy.start()

    wide = iota((rows + 2 * HALO, LANES), 1) < LANES // 2
    for copy in static_halos:
        copy.wait_recv()
    for i in range(7):
        ext[i, :, 0:LANES] = sc[i]
        ext[i, :, LANES:2 * LANES] = jnp.where(wide, sr[i], sl[i])
    for copy in moving_halos:
        copy.wait_recv()
    for c in range(3):
        ext[7 + c, :, 0:LANES] = dc[c]
        ext[7 + c, :, LANES:2 * LANES] = jnp.where(wide, dr[c], dl[c])

    height = rows + 2 * HALO

    def sweep(i, carry):
        for c in range(3):
            p = ext[4 + c]
            new = ext[7 + c] + ext[0] * pltpu.roll(p, 1, 0)
            new = new + ext[1] * pltpu.roll(p, height - 1, 0)
            new = new + ext[2] * pltpu.roll(p, 1, 1)
            new = new + ext[3] * pltpu.roll(p, 2 * LANES - 1, 1)
            ext[4 + c] = new
        return carry

    lax.fori_loop(0, SWEEPS, sweep, 0)

    listed = owner.shape[1]
    owner_f = owner[...].astype(F32)
    picked_col = to_column(picked[...].astype(F32))
    by_owner = (iota((gores, listed), 0).astype(F32) == owner_f).astype(F32)
    before = (iota((listed, listed), 0) < iota((listed, listed), 1)).astype(F32)
    rank = exact_dot(by_owner, before)
    by_row = (iota((listed, rows), 1).astype(F32) == picked_col).astype(F32)
    slots = [jnp.where(rank == float(slot), by_owner, 0.0) for slot in range(2)]
    for c in range(3):
        patch = ext[4 + c, own, 0:LANES]
        canopy_out[c] = patch
        chosen = exact_dot(by_row, patch)
        for slot in range(2):
            csend[pl.ds(3 * slot + c, gores, stride=8), :] = exact_dot(slots[slot], chosen)
    for slot in range(2):
        csend[pl.ds(6 + slot, gores, stride=8), :] = jnp.broadcast_to(
            jnp.sum(slots[slot], axis=1, keepdims=True), (gores, LANES)
        )
    mine = pl.ds(pl.multiple_of(g * 8, 8), 8)
    crecv[mine, :] = csend[mine, :]
    for i in range(1, gores):
        t = lax.rem(g + i, gores)
        pltpu.make_async_remote_copy(
            csend.at[pl.ds(pl.multiple_of(t * 8, 8), 8)], crecv.at[mine],
            con_sem.at[0], con_sem.at[1], device_id=(s, t), device_id_type=MESH,
        ).start()
    most = pl.ds(0, (gores - 1) * 8)
    pltpu.make_async_copy(crecv.at[most], crecv.at[most], con_sem.at[1]).wait()
    sets_out[...] = crecv[...]

    pltpu.make_async_copy(csend.at[most], csend.at[most], con_sem.at[0]).wait()
    wait_all(outbox, 7, 0)
    wait_all(ansbox, 6, 2)
    for copy in static_halos + moving_halos:
        copy.wait_send()

    def drain(i, carry):
        step, c = lax.div(i, 3), lax.rem(i, 3)
        sent_pair(z_copies(step, c), s, slabs)
        sent_pair(y_copies(step, c), g, gores)
        return carry

    lax.fori_loop(0, 3 * STEPS, drain, 0)
    for c in range(3):
        pltpu.make_async_copy(
            v.at[STEPS, c, pl.ds(1, cz)], fluid_out.at[c], store_sem.at[c]
        ).wait()


def contact_kernel(
    gores, fluid_in, canopy_in, sets, fluid_out, canopy_out, force, xj, fj, ft, pad, sem
):
    copies = (
        pltpu.make_async_copy(fluid_in, fluid_out, sem.at[0]),
        pltpu.make_async_copy(canopy_in, canopy_out, sem.at[1]),
    )
    for copy in copies:
        copy.start()
    slots = 2 * gores
    lane = iota((8, LANES), 1)
    pad[...] = jnp.zeros_like(pad)
    for a in range(slots):
        base = (a // 2) * 8
        flag = sets[base + 6 + a % 2:base + 7 + a % 2, :]
        for c in range(3):
            k = c * slots + a
            row = base + 3 * (a % 2) + c
            point = jnp.where(flag > 0.0, sets[row:row + 1, :], FAR)
            pad[k:k + 1, :] = point
            xj[k] = jnp.broadcast_to(point, (8, LANES))
    points_t = pad[...].T
    pad[...] = points_t
    fj[...] = jnp.zeros_like(fj)

    def tile(it, carry):
        at = pl.ds(pl.multiple_of(it * 8, 8), 8)
        column = pad[at, :]
        total = jnp.zeros((8, LANES), F32)
        for a in range(slots - 2):
            xi = [
                jnp.broadcast_to(column[:, c * slots + a:c * slots + a + 1], (8, LANES))
                for c in range(3)
            ]
            acc = [jnp.zeros((8, LANES), F32) for _ in range(3)]
            for b in range(2 * (a // 2) + 2, slots):
                d = [xi[c] - xj[c * slots + b] for c in range(3)]
                square = d[0] * d[0] + d[1] * d[1] + (d[2] * d[2] + SOFTEN)
                inverse = lax.rsqrt(square)
                gap = jnp.maximum(REACH - square * inverse, 0.0)
                weight = gap * gap * inverse
                for c in range(3):
                    push = weight * d[c]
                    acc[c] = acc[c] + push
                    fj[c * slots + b] = fj[c * slots + b] + push
            for c in range(3):
                total = jnp.where(
                    lane == c * slots + a, jnp.sum(acc[c], axis=1, keepdims=True), total
                )
        ft[at, :] = total
        return carry

    lax.fori_loop(0, LANES // 8, tile, 0)
    rows_t = ft[...].T
    for c in range(3):
        for a in range(slots):
            k = c * slots + a
            force[c, a:a + 1, :] = GAIN * (
                rows_t[k:k + 1, :] - jnp.sum(fj[k], axis=0, keepdims=True)
            )
    for copy in copies:
        copy.wait()


def body(
    slabs, gores,
    fluid_velocity, viscosity, pressure_jump, normals, canopy_position, tension,
    slot_cut, couple_dest, couple_block, contact_owner, contact_row,
):
    cz, cy, nx = viscosity.shape
    rows = pressure_jump.shape[0]
    devices = slabs * gores
    zy = cz * cy
    nbx = nx // LANES
    vmem = pl.BlockSpec(memory_space=pltpu.VMEM)
    anywhere = pl.BlockSpec(memory_space=pl.ANY)
    dma = pltpu.SemaphoreType.DMA
    cut_width = min(LANES, slot_cut.shape[0])
    tall = rows + 2 * HALO
    fluid, canopy, sets = pl.pallas_call(
        functools.partial(main_kernel, slabs, gores),
        out_shape=(
            jax.ShapeDtypeStruct(fluid_velocity.shape, F32),
            jax.ShapeDtypeStruct(canopy_position.shape, F32),
            jax.ShapeDtypeStruct((gores * 8, LANES), F32),
        ),
        in_specs=[anywhere, anywhere] + [vmem] * 9,
        out_specs=(anywhere, vmem, vmem),
        scratch_shapes=[
            pltpu.VMEM((STEPS + 1, 3, cz + 2, cy, nx), F32),
            pltpu.VMEM((cz, cy, nx), F32),
            pltpu.VMEM((STEPS, 2, 3, cz, nx), F32),
            pltpu.VMEM((STEPS, 2, 3, cz, nx), F32),
            pltpu.VMEM((devices * 8, LANES), F32),
            pltpu.VMEM((devices * 8, LANES), F32),
            pltpu.VMEM((devices * 8, LANES), F32),
            pltpu.VMEM((devices * 8, LANES), F32),
            pltpu.VMEM((nbx, zy, 2 * devices), BF16),
            pltpu.VMEM((nbx, 2 * devices, zy), BF16),
            pltpu.VMEM((7, tall, LANES), F32),
            pltpu.VMEM((7, tall, LANES), F32),
            pltpu.VMEM((7, tall, LANES), F32),
            pltpu.VMEM((3, tall, LANES), F32),
            pltpu.VMEM((3, tall, LANES), F32),
            pltpu.VMEM((3, tall, LANES), F32),
            pltpu.VMEM((10, tall, 2 * LANES), F32),
            pltpu.VMEM((rows, LANES), F32),
            pltpu.VMEM((gores * 8, LANES), F32),
            pltpu.VMEM((gores * 8, LANES), F32),
            dma((4,)),
            dma((3,)),
            dma((STEPS, 2, 3)),
            dma((STEPS, 2, 3)),
            dma((STEPS, 2, 3)),
            dma((STEPS, 2, 3)),
            dma((4,)),
            dma((16,)),
            dma((16,)),
            dma((2,)),
        ],
        compiler_params=pltpu.CompilerParams(
            collective_id=0, has_side_effects=True, vmem_limit_bytes=56 << 20
        ),
        name="fluid_membrane",
    )(
        fluid_velocity, viscosity, pressure_jump, normals, canopy_position, tension,
        slot_cut.reshape(-1, cut_width),
        couple_dest[0].T, couple_block[0].T, contact_owner[:, :, 0], contact_row,
    )
    slots = 2 * gores
    fluid, canopy, force = pl.pallas_call(
        functools.partial(contact_kernel, gores),
        out_shape=(
            jax.ShapeDtypeStruct(fluid.shape, F32),
            jax.ShapeDtypeStruct(canopy.shape, F32),
            jax.ShapeDtypeStruct((3, slots, LANES), F32),
        ),
        in_specs=[anywhere, anywhere, vmem],
        out_specs=(anywhere, anywhere, vmem),
        scratch_shapes=[
            pltpu.VMEM((3 * slots, 8, LANES), F32),
            pltpu.VMEM((3 * slots, 8, LANES), F32),
            pltpu.VMEM((LANES, LANES), F32),
            pltpu.VMEM((LANES, LANES), F32),
            dma((2,)),
        ],
        name="contact",
    )(fluid, canopy, sets)
    return fluid, canopy, jnp.swapaxes(force, 0, 1)[None, None]


def solution(mesh):
    in_specs = (
        P(None, "slab", "gore", None),
        P("slab", "gore", None),
        P("slab", "gore"),
        P(None, "slab", "gore"),
        P(None, "slab", "gore"),
        P(None, "slab", "gore"),
        P(),
        P("gore", "slab", None),
        P("gore", "slab", None),
        P("gore", "slab", None),
        P("gore", "slab"),
    )
    out_specs = (
        P(None, "slab", "gore", None),
        P(None, "slab", "gore"),
        P("slab", "gore", None, None, None),
    )
    step = functools.partial(body, mesh.shape["slab"], mesh.shape["gore"])
    return jax.shard_map(step, mesh=mesh, in_specs=in_specs, out_specs=out_specs, check_vma=False)
```

```python
import functools

import jax
import jax.numpy as jnp
from jax import lax
from jax.experimental import pallas as pl
from jax.experimental.pallas import tpu as pltpu
from jax.sharding import PartitionSpec as P

STEPS = 3
SWEEPS = 8
HALO = 8
LANES = 128
GAIN = 0.1
REACH = 1.0
SOFTEN = 0.01
FAR = 1.0e15
MESH = pl.DeviceIdType.MESH
F32 = jnp.float32
BF16 = jnp.bfloat16


def iota(shape, dim):
    return lax.broadcasted_iota(jnp.int32, shape, dim)


def dot(a, b):
    return lax.dot_general(a, b, (((1,), (0,)), ((), ())), preferred_element_type=F32)


def exact_dot(a, b):
    return lax.dot_general(
        a, b, (((1,), (0,)), ((), ())),
        precision=lax.Precision.HIGHEST, preferred_element_type=F32,
    )


def split(x):
    hi = x.astype(BF16)
    return hi, (x - hi.astype(F32)).astype(BF16)


def to_column(row):
    n = row.shape[1]
    same = iota((n, n), 0) == iota((n, n), 1)
    return jnp.sum(jnp.where(same, jnp.broadcast_to(row, (n, n)), 0.0), axis=1, keepdims=True)


def main_kernel(
    slabs, gores,
    fluid_hbm, visc_hbm, jump, normals, canopy, tension, cut, dest, block, owner, picked,
    fluid_out, canopy_out, sets_out,
    v, vis, yh, ys, outbox, inbox, ansbox, retbox, hot_t, hot,
    sc, sl, sr, dc, dl, dr, ext, inv, csend, crecv,
    load_sem, store_sem, zs_sem, zr_sem, ysend_sem, yr_sem, a2a_sem, mem_s, mem_r, con_sem,
):
    s = lax.axis_index("slab")
    g = lax.axis_index("gore")
    me = s * gores + g
    devices = slabs * gores
    cz, cy, nx = vis.shape
    zy = cz * cy
    nbx = nx // LANES
    rows = jump.shape[0]

    def device(t):
        return (lax.div(t, gores), lax.rem(t, gores))

    def rows_of(t, count):
        return pl.ds(pl.multiple_of(t * 8, 8), count)

    loads = [
        pltpu.make_async_copy(fluid_hbm.at[c], v.at[0, c, pl.ds(1, cz)], load_sem.at[c])
        for c in range(3)
    ]
    loads.append(pltpu.make_async_copy(visc_hbm, vis, load_sem.at[3]))
    for copy in loads:
        copy.start()
    barrier = pltpu.get_barrier_semaphore()

    def greet(i, carry):
        t = lax.rem(me + i, devices)
        pl.semaphore_signal(barrier, inc=1, device_id=device(t), device_id_type=MESH)
        return carry

    lax.fori_loop(1, devices, greet, 0)

    zero_plane = jnp.zeros((cy, nx), F32)
    zero_edge = jnp.zeros((cz, nx), F32)

    @pl.when(s == 0)
    def _():
        for step in range(STEPS):
            for c in range(3):
                v[step, c, 0] = zero_plane

    @pl.when(s == slabs - 1)
    def _():
        for step in range(STEPS):
            for c in range(3):
                v[step, c, cz + 1] = zero_plane

    @pl.when(g == 0)
    def _():
        for step in range(STEPS):
            for c in range(3):
                yh[step, 0, c] = zero_edge

    @pl.when(g == gores - 1)
    def _():
        for step in range(STEPS):
            for c in range(3):
                yh[step, 1, c] = zero_edge

    dest_row = jnp.concatenate([dest[0:1, :], dest[1:2, :]], axis=1).astype(F32)
    line_row = jnp.concatenate([block[0:1, :], block[1:2, :]], axis=1).astype(F32)
    entries = 2 * rows
    dest_col = to_column(dest_row)
    line_col = to_column(line_row) + 1.0
    by_dev = (iota((devices, entries), 0).astype(F32) == dest_row).astype(F32)
    by_entry = (iota((entries, devices), 1).astype(F32) == dest_col).astype(F32)
    row_a = lax.rem(iota((entries, entries), 0), rows)
    row_b = lax.rem(iota((entries, entries), 1), rows)
    rank_dev = dot(by_dev.astype(BF16), (row_a < row_b).astype(BF16))
    rank_entry = dot((row_b < row_a).astype(BF16), by_entry.astype(BF16))
    surface = [jump[...] * normals[c] * 0.25 for c in range(3)]
    columns = [jnp.concatenate([t, t], axis=0) for t in surface]
    columns.append(jnp.broadcast_to(line_col, (entries, LANES)))
    table = jnp.concatenate(columns, axis=1)
    lines = []
    for slot in range(2):
        pick = jnp.where(rank_dev == float(slot), by_dev, 0.0)
        placed = exact_dot(pick, table)
        for c in range(3):
            outbox[pl.ds(3 * slot + c, devices, stride=8), :] = placed[:, c * LANES:(c + 1) * LANES]
        lines.append(placed[:, 3 * LANES:])
    outbox[pl.ds(6, devices, stride=8), :] = jnp.where(
        iota((devices, LANES), 1) < LANES // 2, lines[0], lines[1]
    )
    back_pick = jnp.concatenate(
        [jnp.where(rank_entry == float(slot), by_entry, 0.0) for slot in range(2)], axis=1
    ).astype(BF16)

    first = s * rows
    cut_f = cut[...].astype(F32)
    cut_rows, cut_width = cut.shape
    node = first + iota((rows, cut_width), 0)
    lane = iota((rows, cut_width), 1)
    down = jnp.zeros((rows, cut_width), F32)
    up = jnp.zeros((rows, cut_width), F32)
    total_rows = slabs * rows
    for q in range(cut_rows):
        index = q * cut_width + lane
        keep = jnp.broadcast_to(1.0 - cut_f[q:q + 1, :], (rows, cut_width))
        down += jnp.where((index == node) & (index < total_rows - 1), keep, 0.0)
        up += jnp.where(index == node - 1, keep, 0.0)
    keep_down = jnp.sum(down, axis=1, keepdims=True)
    keep_up = jnp.sum(up, axis=1, keepdims=True)
    w_up = tension[0] * keep_up
    w_down = tension[1] * keep_down
    w_left = tension[2]
    w_right = tension[3]
    scale = 1.0 / (1.0 + w_up + w_down + w_left + w_right)
    inv[...] = scale
    own = pl.ds(HALO, rows)
    for i, w in enumerate((w_up, w_down, w_left, w_right)):
        sc[i, own, :] = w * scale
    for c in range(3):
        sc[4 + c, own, :] = canopy[c]

    pl.semaphore_wait(barrier, devices - 1)
    inbox[rows_of(me, 8), :] = outbox[rows_of(me, 8), :]

    def send_all(source, target, count, sem):
        def one(i, carry):
            t = lax.rem(me + i, devices)
            pltpu.make_async_remote_copy(
                source.at[rows_of(t, count)], target.at[rows_of(me, count)],
                a2a_sem.at[sem], a2a_sem.at[sem + 1],
                device_id=device(t), device_id_type=MESH,
            ).start()
            return carry

        lax.fori_loop(1, devices, one, 0)

    def wait_all(buffer, count, sem):
        part = buffer.at[pl.ds(0, (devices - 1) * count)]
        pltpu.make_async_copy(part, part, a2a_sem.at[sem]).wait()

    send_all(outbox, inbox, 7, 0)
    wait_all(inbox, 7, 1)

    def z_copies(step, c):
        up_copy = pltpu.make_async_remote_copy(
            v.at[step, c, cz], v.at[step, c, 0], zs_sem.at[step, 0, c], zr_sem.at[step, 0, c],
            device_id=(lax.rem(s + 1, slabs), g), device_id_type=MESH,
        )
        down_copy = pltpu.make_async_remote_copy(
            v.at[step, c, 1], v.at[step, c, cz + 1], zs_sem.at[step, 1, c], zr_sem.at[step, 1, c],
            device_id=(lax.rem(s + slabs - 1, slabs), g), device_id_type=MESH,
        )
        return up_copy, down_copy

    def y_copies(step, c):
        up_copy = pltpu.make_async_remote_copy(
            ys.at[step, 0, c], yh.at[step, 0, c], ysend_sem.at[step, 0, c], yr_sem.at[step, 0, c],
            device_id=(s, lax.rem(g + 1, gores)), device_id_type=MESH,
        )
        down_copy = pltpu.make_async_remote_copy(
            ys.at[step, 1, c], yh.at[step, 1, c], ysend_sem.at[step, 1, c], yr_sem.at[step, 1, c],
            device_id=(s, lax.rem(g + gores - 1, gores)), device_id_type=MESH,
        )
        return up_copy, down_copy

    def start_pair(pair, at, length):
        @pl.when(at < length - 1)
        def _():
            pair[0].start()

        @pl.when(at > 0)
        def _():
            pair[1].start()

    def recv_pair(pair, at, length):
        @pl.when(at > 0)
        def _():
            pair[0].wait_recv()

        @pl.when(at < length - 1)
        def _():
            pair[1].wait_recv()

    def sent_pair(pair, at, length):
        @pl.when(at < length - 1)
        def _():
            pair[0].wait_send()

        @pl.when(at > 0)
        def _():
            pair[1].wait_send()

    meta = inbox[pl.ds(6, devices, stride=8), :]
    meta_t = meta.T
    line_t = jnp.concatenate(
        [meta_t[0:1, :], meta_t[LANES // 2:LANES // 2 + 1, :]], axis=1
    )
    parts = []
    for c in range(3):
        tiles = jnp.concatenate(
            [inbox[pl.ds(3 * slot + c, devices, stride=8), :] for slot in range(2)], axis=0
        )
        parts.append(split(tiles))
    first_line = (iota((zy, 2 * devices), 0) * nbx + 1).astype(F32)
    for c in range(3):
        loads[c].wait()
        for x in range(nbx):
            if c == 0:
                hot_t[x] = jnp.where(line_t == first_line + float(x), 1.0, 0.0).astype(BF16)
            matrix = hot_t[x]
            added = dot(matrix, parts[c][0]) + dot(matrix, parts[c][1])
            cols = pl.ds(x * LANES, LANES)
            here = v[0, c, pl.ds(1, cz), :, cols]
            v[0, c, pl.ds(1, cz), :, cols] = here + added.reshape(cz, cy, LANES)
        start_pair(z_copies(0, c), s, slabs)
        for z in range(cz):
            ys[0, 0, c, z:z + 1, :] = v[0, c, z + 1, cy - 1:cy, :]
            ys[0, 1, c, z:z + 1, :] = v[0, c, z + 1, 0:1, :]
        start_pair(y_copies(0, c), g, gores)
    loads[3].wait()

    def neighbours(mid, left, right, base):
        below, above = lax.rem(s + 1, slabs), lax.rem(s + slabs - 1, slabs)
        after, before = lax.rem(g + 1, gores), lax.rem(g + gores - 1, gores)
        whole = pl.ds(HALO, rows)
        head = pl.ds(HALO, HALO)
        tail = pl.ds(rows, HALO)
        over = pl.ds(0, HALO)
        under = pl.ds(rows + HALO, HALO)
        plan = (
            (whole, left, whole, (s, after)),
            (whole, right, whole, (s, before)),
            (tail, mid, over, (below, g)),
            (head, mid, under, (above, g)),
            (tail, left, over, (below, after)),
            (tail, right, over, (below, before)),
            (head, left, under, (above, after)),
            (head, right, under, (above, before)),
        )
        return [
            pltpu.make_async_remote_copy(
                mid.at[:, src], to.at[:, dst], mem_s.at[base + i], mem_r.at[base + i],
                device_id=where, device_id_type=MESH,
            )
            for i, (src, to, dst, where) in enumerate(plan)
        ]

    static_halos = neighbours(sc, sl, sr, 0)
    for copy in static_halos:
        copy.start()

    at_line = (iota((devices, zy), 1) * nbx + 1).astype(F32)
    for slot in range(2):
        named = jnp.broadcast_to(
            meta[:, slot * (LANES // 2):slot * (LANES // 2) + 1], (devices, zy)
        )
        for x in range(nbx):
            hot[x, slot * devices:(slot + 1) * devices, :] = jnp.where(
                named == at_line + float(x), 1.0, 0.0
            ).astype(BF16)

    sub = iota((8, nx), 0)
    lan = iota((8, nx), 1)

    def plane(step, c, z, stage):
        blocks = cy // 8
        center = v[step, c, z + 1, pl.ds(0, 8), :]
        up_roll = jnp.broadcast_to(yh[step, 0, c, pl.ds(z, 1), :], (8, nx))
        down_roll = pltpu.roll(center, 7, 0)
        for yb in range(blocks):
            at = pl.ds(8 * yb, 8)
            rolled = pltpu.roll(center, 1, 0)
            upper = jnp.where(sub == 0, up_roll, rolled)
            if yb + 1 < blocks:
                following = v[step, c, z + 1, pl.ds(8 * yb + 8, 8), :]
                next_roll = pltpu.roll(following, 7, 0)
            else:
                following = None
                next_roll = jnp.broadcast_to(yh[step, 1, c, pl.ds(z, 1), :], (8, nx))
            lower = jnp.where(sub == 7, next_roll, down_roll)
            total = v[step, c, z, at, :] + v[step, c, z + 2, at, :]
            total = total + upper + lower
            total = total + jnp.where(lan == 0, 0.0, pltpu.roll(center, 1, 1))
            total = total + jnp.where(lan == nx - 1, 0.0, pltpu.roll(center, nx - 1, 1))
            new = center + vis[z, at, :] * (total - 6.0 * center)
            v[step + 1, c, z + 1, at, :] = new
            if stage and yb == 0:
                ys[step + 1, 1, c, pl.ds(z, 1), :] = new[0:1, :]
            if stage and yb == blocks - 1:
                ys[step + 1, 0, c, pl.ds(z, 1), :] = new[7:8, :]
            center, up_roll, down_roll = following, rolled, next_roll

    def substep(step, c, stage):
        recv_pair(z_copies(step, c), s, slabs)
        recv_pair(y_copies(step, c), g, gores)
        plane(step, c, 0, stage)
        plane(step, c, cz - 1, stage)
        if stage:
            start_pair(z_copies(step + 1, c), s, slabs)

        def inner(z, carry):
            plane(step, c, z, stage)
            return carry

        lax.fori_loop(1, cz - 1, inner, 0)
        if stage:
            start_pair(y_copies(step + 1, c), g, gores)

    def early(i, carry):
        substep(lax.div(i, 3), lax.rem(i, 3), True)
        return carry

    lax.fori_loop(0, 3 * (STEPS - 1), early, 0)

    def last(c, carry):
        substep(STEPS - 1, c, False)
        pltpu.make_async_copy(
            v.at[STEPS, c, pl.ds(1, cz)], fluid_out.at[c], store_sem.at[c]
        ).start()
        sampled = jnp.zeros((2 * devices, LANES), F32)
        for x in range(nbx):
            cell = v[STEPS, c, pl.ds(1, cz), :, pl.ds(x * LANES, LANES)].reshape(zy, LANES)
            hi, lo = split(cell)
            sampled = sampled + dot(hot[x], hi) + dot(hot[x], lo)
        for slot in range(2):
            ansbox[pl.ds(3 * slot + c, devices, stride=8), :] = (
                sampled[slot * devices:(slot + 1) * devices]
            )
        return carry

    lax.fori_loop(0, 3, last, 0)

    retbox[rows_of(me, 8), :] = ansbox[rows_of(me, 8), :]
    send_all(ansbox, retbox, 6, 2)
    wait_all(retbox, 6, 3)
    for c in range(3):
        hi, lo = split(
            jnp.concatenate(
                [retbox[pl.ds(3 * slot + c, devices, stride=8), :] for slot in range(2)], axis=0
            )
        )
        taken = dot(back_pick, hi) + dot(back_pick, lo)
        node_velocity = (taken[:rows] + taken[rows:]) * 0.5
        dc[c, own, :] = (canopy[c] + node_velocity) * inv[...]

    moving_halos = neighbours(dc, dl, dr, 8)
    for copy in moving_halos:
        copy.start()

    wide = iota((rows + 2 * HALO, LANES), 1) < LANES // 2
    for copy in static_halos:
        copy.wait_recv()
    for i in range(7):
        ext[i, :, 0:LANES] = sc[i]
        ext[i, :, LANES:2 * LANES] = jnp.where(wide, sr[i], sl[i])
    for copy in moving_halos:
        copy.wait_recv()
    for c in range(3):
        ext[7 + c, :, 0:LANES] = dc[c]
        ext[7 + c, :, LANES:2 * LANES] = jnp.where(wide, dr[c], dl[c])

    height = rows + 2 * HALO

    def sweep(i, carry):
        for c in range(3):
            p = ext[4 + c]
            new = ext[7 + c] + ext[0] * pltpu.roll(p, 1, 0)
            new = new + ext[1] * pltpu.roll(p, height - 1, 0)
            new = new + ext[2] * pltpu.roll(p, 1, 1)
            new = new + ext[3] * pltpu.roll(p, 2 * LANES - 1, 1)
            ext[4 + c] = new
        return carry

    lax.fori_loop(0, SWEEPS, sweep, 0)

    listed = owner.shape[1]
    owner_f = owner[...].astype(F32)
    picked_col = to_column(picked[...].astype(F32))
    by_owner = (iota((gores, listed), 0).astype(F32) == owner_f).astype(F32)
    before = (iota((listed, listed), 0) < iota((listed, listed), 1)).astype(F32)
    rank = exact_dot(by_owner, before)
    by_row = (iota((listed, rows), 1).astype(F32) == picked_col).astype(F32)
    slots = [jnp.where(rank == float(slot), by_owner, 0.0) for slot in range(2)]
    for c in range(3):
        patch = ext[4 + c, own, 0:LANES]
        canopy_out[c] = patch
        chosen = exact_dot(by_row, patch)
        for slot in range(2):
            csend[pl.ds(3 * slot + c, gores, stride=8), :] = exact_dot(slots[slot], chosen)
    for slot in range(2):
        csend[pl.ds(6 + slot, gores, stride=8), :] = jnp.broadcast_to(
            jnp.sum(slots[slot], axis=1, keepdims=True), (gores, LANES)
        )
    mine = pl.ds(pl.multiple_of(g * 8, 8), 8)
    crecv[mine, :] = csend[mine, :]
    for i in range(1, gores):
        t = lax.rem(g + i, gores)
        pltpu.make_async_remote_copy(
            csend.at[pl.ds(pl.multiple_of(t * 8, 8), 8)], crecv.at[mine],
            con_sem.at[0], con_sem.at[1], device_id=(s, t), device_id_type=MESH,
        ).start()
    most = pl.ds(0, (gores - 1) * 8)
    pltpu.make_async_copy(crecv.at[most], crecv.at[most], con_sem.at[1]).wait()
    sets_out[...] = crecv[...]

    pltpu.make_async_copy(csend.at[most], csend.at[most], con_sem.at[0]).wait()
    wait_all(outbox, 7, 0)
    wait_all(ansbox, 6, 2)
    for copy in static_halos + moving_halos:
        copy.wait_send()

    def drain(i, carry):
        step, c = lax.div(i, 3), lax.rem(i, 3)
        sent_pair(z_copies(step, c), s, slabs)
        sent_pair(y_copies(step, c), g, gores)
        return carry

    lax.fori_loop(0, 3 * STEPS, drain, 0)
    for c in range(3):
        pltpu.make_async_copy(
            v.at[STEPS, c, pl.ds(1, cz)], fluid_out.at[c], store_sem.at[c]
        ).wait()


def contact_kernel(
    gores, fluid_in, canopy_in, sets, fluid_out, canopy_out, force, xj, fj, acc_ref, pad, field, sem
):
    load = pltpu.make_async_copy(fluid_in, field, sem.at[0])
    store = pltpu.make_async_copy(field, fluid_out, sem.at[1])
    load.start()
    canopy_out[...] = canopy_in[...]
    slots = 2 * gores
    group = 8
    pad[...] = jnp.zeros_like(pad)
    for a in range(slots):
        base = (a // 2) * 8
        flag = sets[base + 6 + a % 2:base + 7 + a % 2, :]
        for c in range(3):
            k = c * slots + a
            row = base + 3 * (a % 2) + c
            point = jnp.where(flag > 0.0, sets[row:row + 1, :], FAR)
            pad[k:k + 1, :] = point
            xj[k] = jnp.broadcast_to(point, (8, LANES))
    points_t = pad[...].T
    pad[...] = points_t
    fj[...] = jnp.zeros_like(fj)

    def block(i, carry):
        at = [pl.ds(pl.multiple_of((i * group + t) * 8, 8), 8) for t in range(group)]
        column = [pad[rows, :] for rows in at]
        for a in range(slots - 2):
            xi = [
                [
                    jnp.broadcast_to(
                        column[t][:, c * slots + a:c * slots + a + 1], (8, LANES)
                    )
                    for c in range(3)
                ]
                for t in range(group)
            ]
            acc = [[None] * 3 for _ in range(group)]
            for b in range(2 * (a // 2) + 2, slots):
                other = [xj[c * slots + b] for c in range(3)]
                pushed = [None] * 3
                for t in range(group):
                    d = [xi[t][c] - other[c] for c in range(3)]
                    square = d[0] * d[0] + d[1] * d[1] + (d[2] * d[2] + SOFTEN)
                    inverse = lax.rsqrt(square)
                    gap = jnp.maximum(REACH - square * inverse, 0.0)
                    weight = gap * gap * inverse
                    for c in range(3):
                        push = weight * d[c]
                        acc[t][c] = push if acc[t][c] is None else acc[t][c] + push
                        pushed[c] = push if pushed[c] is None else pushed[c] + push
                for c in range(3):
                    fj[c * slots + b] = fj[c * slots + b] + pushed[c]
            for t in range(group):
                for c in range(3):
                    acc_ref[c * slots + a, at[t], :] = acc[t][c]

        @pl.when(i == 0)
        def _():
            load.wait()
            store.start()

        return carry

    lax.fori_loop(0, LANES // (8 * group), block, 0)
    for c in range(3):
        for a in range(slots):
            k = c * slots + a
            total = -jnp.sum(fj[k], axis=0, keepdims=True)
            if a < slots - 2:
                total = total + jnp.sum(acc_ref[k].T, axis=0, keepdims=True)
            force[c, a:a + 1, :] = GAIN * total
    store.wait()


def body(
    slabs, gores,
    fluid_velocity, viscosity, pressure_jump, normals, canopy_position, tension,
    slot_cut, couple_dest, couple_block, contact_owner, contact_row,
):
    cz, cy, nx = viscosity.shape
    rows = pressure_jump.shape[0]
    devices = slabs * gores
    zy = cz * cy
    nbx = nx // LANES
    vmem = pl.BlockSpec(memory_space=pltpu.VMEM)
    anywhere = pl.BlockSpec(memory_space=pl.ANY)
    dma = pltpu.SemaphoreType.DMA
    cut_width = min(LANES, slot_cut.shape[0])
    tall = rows + 2 * HALO
    fluid, canopy, sets = pl.pallas_call(
        functools.partial(main_kernel, slabs, gores),
        out_shape=(
            jax.ShapeDtypeStruct(fluid_velocity.shape, F32),
            jax.ShapeDtypeStruct(canopy_position.shape, F32),
            jax.ShapeDtypeStruct((gores * 8, LANES), F32),
        ),
        in_specs=[anywhere, anywhere] + [vmem] * 9,
        out_specs=(anywhere, vmem, vmem),
        scratch_shapes=[
            pltpu.VMEM((STEPS + 1, 3, cz + 2, cy, nx), F32),
            pltpu.VMEM((cz, cy, nx), F32),
            pltpu.VMEM((STEPS, 2, 3, cz, nx), F32),
            pltpu.VMEM((STEPS, 2, 3, cz, nx), F32),
            pltpu.VMEM((devices * 8, LANES), F32),
            pltpu.VMEM((devices * 8, LANES), F32),
            pltpu.VMEM((devices * 8, LANES), F32),
            pltpu.VMEM((devices * 8, LANES), F32),
            pltpu.VMEM((nbx, zy, 2 * devices), BF16),
            pltpu.VMEM((nbx, 2 * devices, zy), BF16),
            pltpu.VMEM((7, tall, LANES), F32),
            pltpu.VMEM((7, tall, LANES), F32),
            pltpu.VMEM((7, tall, LANES), F32),
            pltpu.VMEM((3, tall, LANES), F32),
            pltpu.VMEM((3, tall, LANES), F32),
            pltpu.VMEM((3, tall, LANES), F32),
            pltpu.VMEM((10, tall, 2 * LANES), F32),
            pltpu.VMEM((rows, LANES), F32),
            pltpu.VMEM((gores * 8, LANES), F32),
            pltpu.VMEM((gores * 8, LANES), F32),
            dma((4,)),
            dma((3,)),
            dma((STEPS, 2, 3)),
            dma((STEPS, 2, 3)),
            dma((STEPS, 2, 3)),
            dma((STEPS, 2, 3)),
            dma((4,)),
            dma((16,)),
            dma((16,)),
            dma((2,)),
        ],
        compiler_params=pltpu.CompilerParams(
            collective_id=0, has_side_effects=True, vmem_limit_bytes=56 << 20
        ),
        name="fluid_membrane",
    )(
        fluid_velocity, viscosity, pressure_jump, normals, canopy_position, tension,
        slot_cut.reshape(-1, cut_width),
        couple_dest[0].T, couple_block[0].T, contact_owner[:, :, 0], contact_row,
    )
    slots = 2 * gores
    fluid, canopy, force = pl.pallas_call(
        functools.partial(contact_kernel, gores),
        out_shape=(
            jax.ShapeDtypeStruct(fluid.shape, F32),
            jax.ShapeDtypeStruct(canopy.shape, F32),
            jax.ShapeDtypeStruct((3, slots, LANES), F32),
        ),
        in_specs=[anywhere, vmem, vmem],
        out_specs=(anywhere, vmem, vmem),
        scratch_shapes=[
            pltpu.VMEM((3 * slots, 8, LANES), F32),
            pltpu.VMEM((3 * slots, 8, LANES), F32),
            pltpu.VMEM((3 * slots, LANES, LANES), F32),
            pltpu.VMEM((LANES, LANES), F32),
            pltpu.VMEM(fluid.shape, F32),
            dma((2,)),
        ],
        name="contact",
    )(fluid, canopy, sets)
    return fluid, canopy, jnp.swapaxes(force, 0, 1)[None, None]


def solution(mesh):
    in_specs = (
        P(None, "slab", "gore", None),
        P("slab", "gore", None),
        P("slab", "gore"),
        P(None, "slab", "gore"),
        P(None, "slab", "gore"),
        P(None, "slab", "gore"),
        P(),
        P("gore", "slab", None),
        P("gore", "slab", None),
        P("gore", "slab", None),
        P("gore", "slab"),
    )
    out_specs = (
        P(None, "slab", "gore", None),
        P(None, "slab", "gore"),
        P("slab", "gore", None, None, None),
    )
    step = functools.partial(body, mesh.shape["slab"], mesh.shape["gore"])
    return jax.shard_map(step, mesh=mesh, in_specs=in_specs, out_specs=out_specs, check_vma=False)
```

```python
import functools

import jax
import jax.numpy as jnp
from jax import lax
from jax.experimental import pallas as pl
from jax.experimental.pallas import tpu as pltpu
from jax.sharding import PartitionSpec as P

STEPS = 3
SWEEPS = 8
HALO = 8
LANES = 128
GAIN = 0.1
REACH = 1.0
SOFTEN = 0.01
FAR = 1.0e15
MESH = pl.DeviceIdType.MESH
F32 = jnp.float32
BF16 = jnp.bfloat16


def iota(shape, dim):
    return lax.broadcasted_iota(jnp.int32, shape, dim)


def dot(a, b):
    return lax.dot_general(a, b, (((1,), (0,)), ((), ())), preferred_element_type=F32)


def exact_dot(a, b):
    return lax.dot_general(
        a, b, (((1,), (0,)), ((), ())),
        precision=lax.Precision.HIGHEST, preferred_element_type=F32,
    )


def split(x):
    hi = x.astype(BF16)
    return hi, (x - hi.astype(F32)).astype(BF16)


def to_column(row):
    n = row.shape[1]
    same = iota((n, n), 0) == iota((n, n), 1)
    return jnp.sum(jnp.where(same, jnp.broadcast_to(row, (n, n)), 0.0), axis=1, keepdims=True)


def main_kernel(
    slabs, gores,
    fluid_hbm, visc_hbm, jump_hbm, normals_hbm, canopy_hbm, tension_hbm, cut_hbm,
    dest_hbm, block_hbm, owner_hbm, picked_hbm,
    fluid_out, canopy_out, sets_out,
    jump, normals, canopy, tension, cut, dest, block, owner, picked,
    v, vis, yh, ys, outbox, inbox, ansbox, retbox, hot_t, hot,
    sc, spr, spl, sl, sr, dc, dpr, dpl, dl, dr, ext, inv, csend, crecv,
    small_sem, load_sem, store_sem, zs_sem, zr_sem, ysend_sem, yr_sem, a2a_sem, mem_s, mem_r, con_sem,
):
    s = lax.axis_index("slab")
    g = lax.axis_index("gore")
    me = s * gores + g
    devices = slabs * gores
    cz, cy, nx = vis.shape
    zy = cz * cy
    nbx = nx // LANES
    rows = jump.shape[0]

    def device(t):
        return (lax.div(t, gores), lax.rem(t, gores))

    def rows_of(t, count):
        return pl.ds(pl.multiple_of(t * 8, 8), count)

    loads = [
        pltpu.make_async_copy(fluid_hbm.at[c], v.at[0, c, pl.ds(1, cz)], load_sem.at[c])
        for c in range(3)
    ]
    loads.append(pltpu.make_async_copy(visc_hbm, vis, load_sem.at[3]))
    small = [
        pltpu.make_async_copy(src, dst, small_sem.at[i])
        for i, (src, dst) in enumerate((
            (dest_hbm, dest), (block_hbm, block), (jump_hbm, jump), (normals_hbm, normals),
            (canopy_hbm, canopy), (tension_hbm, tension), (cut_hbm, cut),
            (owner_hbm, owner), (picked_hbm, picked),
        ))
    ]
    for copy in small + loads:
        copy.start()
    barrier = pltpu.get_barrier_semaphore()

    def greet(i, carry):
        t = lax.rem(me + i, devices)
        pl.semaphore_signal(barrier, inc=1, device_id=device(t), device_id_type=MESH)
        return carry

    lax.fori_loop(1, devices, greet, 0)

    for copy in small:
        copy.wait()

    dest_row = jnp.concatenate([dest[0:1, :], dest[1:2, :]], axis=1).astype(F32)
    line_row = jnp.concatenate([block[0:1, :], block[1:2, :]], axis=1).astype(F32)
    entries = 2 * rows
    dest_col = to_column(dest_row)
    line_col = to_column(line_row) + 1.0
    by_dev = (iota((devices, entries), 0).astype(F32) == dest_row).astype(F32)
    by_entry = (iota((entries, devices), 1).astype(F32) == dest_col).astype(F32)
    row_a = lax.rem(iota((entries, entries), 0), rows)
    row_b = lax.rem(iota((entries, entries), 1), rows)
    rank_dev = dot(by_dev.astype(BF16), (row_a < row_b).astype(BF16))
    rank_entry = dot((row_b < row_a).astype(BF16), by_entry.astype(BF16))
    surface = [jump[...] * normals[c] * 0.25 for c in range(3)]
    columns = [jnp.concatenate([t, t], axis=0) for t in surface]
    columns.append(jnp.broadcast_to(line_col, (entries, LANES)))
    table = jnp.concatenate(columns, axis=1)
    table_hi, table_lo = split(table)
    pick = jnp.concatenate(
        [jnp.where(rank_dev == float(slot), by_dev, 0.0) for slot in range(2)], axis=0
    ).astype(BF16)
    placed = dot(pick, table_hi) + dot(pick, table_lo)
    for slot in range(2):
        for c in range(3):
            outbox[pl.ds(3 * slot + c, devices, stride=8), :] = (
                placed[slot * devices:(slot + 1) * devices, c * LANES:(c + 1) * LANES]
            )
    outbox[pl.ds(6, devices, stride=8), :] = jnp.where(
        iota((devices, LANES), 1) < LANES // 2,
        placed[:devices, 3 * LANES:], placed[devices:, 3 * LANES:],
    )
    back_pick = jnp.concatenate(
        [jnp.where(rank_entry == float(slot), by_entry, 0.0) for slot in range(2)], axis=1
    ).astype(BF16)

    pl.semaphore_wait(barrier, devices - 1)
    inbox[rows_of(me, 8), :] = outbox[rows_of(me, 8), :]

    def send_all(source, target, count, sem):
        def one(i, carry):
            t = lax.rem(me + i, devices)
            pltpu.make_async_remote_copy(
                source.at[rows_of(t, count)], target.at[rows_of(me, count)],
                a2a_sem.at[sem], a2a_sem.at[sem + 1],
                device_id=device(t), device_id_type=MESH,
            ).start()
            return carry

        lax.fori_loop(1, devices, one, 0)

    def wait_all(buffer, count, sem):
        part = buffer.at[pl.ds(0, (devices - 1) * count)]
        pltpu.make_async_copy(part, part, a2a_sem.at[sem]).wait()

    send_all(outbox, inbox, 7, 0)

    zero_plane = jnp.zeros((cy, nx), F32)
    zero_edge = jnp.zeros((cz, nx), F32)

    @pl.when(s == 0)
    def _():
        for step in range(STEPS):
            for c in range(3):
                v[step, c, 0] = zero_plane

    @pl.when(s == slabs - 1)
    def _():
        for step in range(STEPS):
            for c in range(3):
                v[step, c, cz + 1] = zero_plane

    @pl.when(g == 0)
    def _():
        for step in range(STEPS):
            for c in range(3):
                yh[step, 0, c] = zero_edge

    @pl.when(g == gores - 1)
    def _():
        for step in range(STEPS):
            for c in range(3):
                yh[step, 1, c] = zero_edge

    first = s * rows
    cut_f = cut[...].astype(F32)
    cut_rows, cut_width = cut.shape
    node = first + iota((rows, cut_width), 0)
    lane = iota((rows, cut_width), 1)
    down = jnp.zeros((rows, cut_width), F32)
    up = jnp.zeros((rows, cut_width), F32)
    total_rows = slabs * rows
    for q in range(cut_rows):
        index = q * cut_width + lane
        keep = jnp.broadcast_to(1.0 - cut_f[q:q + 1, :], (rows, cut_width))
        down += jnp.where((index == node) & (index < total_rows - 1), keep, 0.0)
        up += jnp.where(index == node - 1, keep, 0.0)
    keep_down = jnp.sum(down, axis=1, keepdims=True)
    keep_up = jnp.sum(up, axis=1, keepdims=True)
    w_up = tension[0] * keep_up
    w_down = tension[1] * keep_down
    w_left = tension[2]
    w_right = tension[3]
    scale = 1.0 / (1.0 + w_up + w_down + w_left + w_right)
    inv[...] = scale
    own = pl.ds(HALO, rows)
    for i, w in enumerate((w_up, w_down, w_left, w_right)):
        sc[i, own, :] = w * scale
    for c in range(3):
        sc[4 + c, own, :] = canopy[c]

    wait_all(inbox, 7, 1)

    def z_copies(step, c):
        up_copy = pltpu.make_async_remote_copy(
            v.at[step, c, cz], v.at[step, c, 0], zs_sem.at[step, 0, c], zr_sem.at[step, 0, c],
            device_id=(lax.rem(s + 1, slabs), g), device_id_type=MESH,
        )
        down_copy = pltpu.make_async_remote_copy(
            v.at[step, c, 1], v.at[step, c, cz + 1], zs_sem.at[step, 1, c], zr_sem.at[step, 1, c],
            device_id=(lax.rem(s + slabs - 1, slabs), g), device_id_type=MESH,
        )
        return up_copy, down_copy

    def y_copies(step, c):
        up_copy = pltpu.make_async_remote_copy(
            ys.at[step, 0, c], yh.at[step, 0, c], ysend_sem.at[step, 0, c], yr_sem.at[step, 0, c],
            device_id=(s, lax.rem(g + 1, gores)), device_id_type=MESH,
        )
        down_copy = pltpu.make_async_remote_copy(
            ys.at[step, 1, c], yh.at[step, 1, c], ysend_sem.at[step, 1, c], yr_sem.at[step, 1, c],
            device_id=(s, lax.rem(g + gores - 1, gores)), device_id_type=MESH,
        )
        return up_copy, down_copy

    def start_pair(pair, at, length):
        @pl.when(at < length - 1)
        def _():
            pair[0].start()

        @pl.when(at > 0)
        def _():
            pair[1].start()

    def recv_pair(pair, at, length):
        @pl.when(at > 0)
        def _():
            pair[0].wait_recv()

        @pl.when(at < length - 1)
        def _():
            pair[1].wait_recv()

    def sent_pair(pair, at, length):
        @pl.when(at < length - 1)
        def _():
            pair[0].wait_send()

        @pl.when(at > 0)
        def _():
            pair[1].wait_send()

    meta = inbox[pl.ds(6, devices, stride=8), :]
    meta_t = meta.T
    line_t = jnp.concatenate(
        [meta_t[0:1, :], meta_t[LANES // 2:LANES // 2 + 1, :]], axis=1
    )
    parts = []
    for c in range(3):
        tiles = jnp.concatenate(
            [inbox[pl.ds(3 * slot + c, devices, stride=8), :] for slot in range(2)], axis=0
        )
        parts.append(jnp.concatenate(split(tiles), axis=1))
    first_line = (iota((zy, 2 * devices), 0) * nbx + 1).astype(F32)
    for c in range(3):
        loads[c].wait()
        for x in range(nbx):
            if c == 0:
                hot_t[x] = jnp.where(line_t == first_line + float(x), 1.0, 0.0).astype(BF16)
            matrix = hot_t[x]
            added = dot(matrix, parts[c])
            added = added[:, :LANES] + added[:, LANES:]
            cols = pl.ds(x * LANES, LANES)
            here = v[0, c, pl.ds(1, cz), :, cols]
            v[0, c, pl.ds(1, cz), :, cols] = here + added.reshape(cz, cy, LANES)
        start_pair(z_copies(0, c), s, slabs)
        for z in range(cz):
            ys[0, 0, c, z:z + 1, :] = v[0, c, z + 1, cy - 1:cy, :]
            ys[0, 1, c, z:z + 1, :] = v[0, c, z + 1, 0:1, :]
        start_pair(y_copies(0, c), g, gores)
    loads[3].wait()

    def neighbours(mid, to_right, to_left, left, right, base):
        below, above = lax.rem(s + 1, slabs), lax.rem(s + slabs - 1, slabs)
        after, before = lax.rem(g + 1, gores), lax.rem(g + gores - 1, gores)
        over, under = pl.ds(0, HALO), pl.ds(rows + HALO, HALO)
        head, tail = pl.ds(0, HALO), pl.ds(rows - HALO, HALO)
        plan = (
            (to_right, left.at[own], (s, after)),
            (to_left, right.at[own], (s, before)),
            (mid.at[:, pl.ds(rows, HALO)], mid.at[:, over], (below, g)),
            (mid.at[:, pl.ds(HALO, HALO)], mid.at[:, under], (above, g)),
            (to_right.at[tail], left.at[over], (below, after)),
            (to_left.at[tail], right.at[over], (below, before)),
            (to_right.at[head], left.at[under], (above, after)),
            (to_left.at[head], right.at[under], (above, before)),
        )
        return [
            pltpu.make_async_remote_copy(
                src, to, mem_s.at[base + i], mem_r.at[base + i],
                device_id=where, device_id_type=MESH,
            )
            for i, (src, to, where) in enumerate(plan)
        ]

    band = lax.div(iota((rows, LANES), 1), HALO)

    def pack(mid, to_right, to_left, count):
        going_right = jnp.zeros((rows, LANES), F32)
        going_left = jnp.zeros((rows, LANES), F32)
        for i in range(count):
            part = mid[i, own, :]
            going_right = jnp.where(
                band == i, pltpu.roll(part, HALO * (i + 1), 1), going_right
            )
            moved = part if i == 0 else pltpu.roll(part, HALO * i, 1)
            going_left = jnp.where(band == i, moved, going_left)
        to_right[...] = going_right
        to_left[...] = going_left

    wide = iota((rows + 2 * HALO, LANES), 1)

    def unpack(mid, left, right, i):
        from_left = pltpu.roll(left[...], LANES - HALO * (i + 1), 1)
        from_right = right[...] if i == 0 else pltpu.roll(right[...], LANES - HALO * i, 1)
        side = jnp.where(wide < HALO, from_right, 0.0)
        side = jnp.where(wide >= LANES - HALO, from_left, side)
        return mid[i], side

    pack(sc, spr, spl, 7)
    static_halos = neighbours(sc, spr, spl, sl, sr, 0)

    at_line = (iota((devices, zy), 1) * nbx + 1).astype(F32)
    for slot in range(2):
        named = jnp.broadcast_to(
            meta[:, slot * (LANES // 2):slot * (LANES // 2) + 1], (devices, zy)
        )
        for x in range(nbx):
            hot[x, slot * devices:(slot + 1) * devices, :] = jnp.where(
                named == at_line + float(x), 1.0, 0.0
            ).astype(BF16)

    sub = iota((8, nx), 0)
    lan = iota((8, nx), 1)

    def plane(step, c, z, stage):
        blocks = cy // 8
        center = v[step, c, z + 1, pl.ds(0, 8), :]
        up_roll = jnp.broadcast_to(yh[step, 0, c, pl.ds(z, 1), :], (8, nx))
        down_roll = pltpu.roll(center, 7, 0)
        for yb in range(blocks):
            at = pl.ds(8 * yb, 8)
            rolled = pltpu.roll(center, 1, 0)
            upper = jnp.where(sub == 0, up_roll, rolled)
            if yb + 1 < blocks:
                following = v[step, c, z + 1, pl.ds(8 * yb + 8, 8), :]
                next_roll = pltpu.roll(following, 7, 0)
            else:
                following = None
                next_roll = jnp.broadcast_to(yh[step, 1, c, pl.ds(z, 1), :], (8, nx))
            lower = jnp.where(sub == 7, next_roll, down_roll)
            total = v[step, c, z, at, :] + v[step, c, z + 2, at, :]
            total = total + upper + lower
            total = total + jnp.where(lan == 0, 0.0, pltpu.roll(center, 1, 1))
            total = total + jnp.where(lan == nx - 1, 0.0, pltpu.roll(center, nx - 1, 1))
            new = center + vis[z, at, :] * (total - 6.0 * center)
            v[step + 1, c, z + 1, at, :] = new
            if stage and yb == 0:
                ys[step + 1, 1, c, pl.ds(z, 1), :] = new[0:1, :]
            if stage and yb == blocks - 1:
                ys[step + 1, 0, c, pl.ds(z, 1), :] = new[7:8, :]
            center, up_roll, down_roll = following, rolled, next_roll

    def substep(step, c, stage):
        recv_pair(y_copies(step, c), g, gores)

        def inner(z, carry):
            plane(step, c, z, stage)
            return carry

        lax.fori_loop(1, cz - 1, inner, 0)
        recv_pair(z_copies(step, c), s, slabs)
        plane(step, c, 0, stage)
        plane(step, c, cz - 1, stage)
        if stage:
            start_pair(z_copies(step + 1, c), s, slabs)
            start_pair(y_copies(step + 1, c), g, gores)

    def early(i, carry):
        substep(lax.div(i, 3), lax.rem(i, 3), True)
        return carry

    lax.fori_loop(0, 3 * (STEPS - 1), early, 0)
    for copy in static_halos:
        copy.start()

    def last(c, carry):
        substep(STEPS - 1, c, False)
        pltpu.make_async_copy(
            v.at[STEPS, c, pl.ds(1, cz)], fluid_out.at[c], store_sem.at[c]
        ).start()
        sampled = jnp.zeros((2 * devices, 2 * LANES), F32)
        for x in range(nbx):
            cell = v[STEPS, c, pl.ds(1, cz), :, pl.ds(x * LANES, LANES)].reshape(zy, LANES)
            sampled = sampled + dot(hot[x], jnp.concatenate(split(cell), axis=1))
        sampled = sampled[:, :LANES] + sampled[:, LANES:]
        for slot in range(2):
            ansbox[pl.ds(3 * slot + c, devices, stride=8), :] = (
                sampled[slot * devices:(slot + 1) * devices]
            )
        return carry

    lax.fori_loop(0, 3, last, 0)

    retbox[rows_of(me, 8), :] = ansbox[rows_of(me, 8), :]
    send_all(ansbox, retbox, 6, 2)
    wait_all(retbox, 6, 3)
    for c in range(3):
        hi, lo = split(
            jnp.concatenate(
                [retbox[pl.ds(3 * slot + c, devices, stride=8), :] for slot in range(2)], axis=0
            )
        )
        taken = dot(back_pick, hi) + dot(back_pick, lo)
        node_velocity = (taken[:rows] + taken[rows:]) * 0.5
        dc[c, own, :] = (canopy[c] + node_velocity) * inv[...]

    pack(dc, dpr, dpl, 3)
    moving_halos = neighbours(dc, dpr, dpl, dl, dr, 8)
    for copy in moving_halos:
        copy.start()

    for copy in static_halos:
        copy.wait_recv()
    for i in range(7):
        middle, side = unpack(sc, sl, sr, i)
        ext[i, :, 0:LANES] = middle
        ext[i, :, LANES:2 * LANES] = side
    for copy in moving_halos:
        copy.wait_recv()
    for c in range(3):
        middle, side = unpack(dc, dl, dr, c)
        ext[7 + c, :, 0:LANES] = middle
        ext[7 + c, :, LANES:2 * LANES] = side

    height = rows + 2 * HALO

    def sweep(i, carry):
        for c in range(3):
            p = ext[4 + c]
            new = ext[7 + c] + ext[0] * pltpu.roll(p, 1, 0)
            new = new + ext[1] * pltpu.roll(p, height - 1, 0)
            new = new + ext[2] * pltpu.roll(p, 1, 1)
            new = new + ext[3] * pltpu.roll(p, 2 * LANES - 1, 1)
            ext[4 + c] = new
        return carry

    lax.fori_loop(0, SWEEPS, sweep, 0)

    listed = owner.shape[1]
    owner_f = owner[...].astype(F32)
    picked_col = to_column(picked[...].astype(F32))
    by_owner = (iota((gores, listed), 0).astype(F32) == owner_f).astype(F32)
    before = (iota((listed, listed), 0) < iota((listed, listed), 1)).astype(F32)
    rank = exact_dot(by_owner, before)
    by_row = (iota((listed, rows), 1).astype(F32) == picked_col).astype(F32)
    slots = [jnp.where(rank == float(slot), by_owner, 0.0) for slot in range(2)]
    for c in range(3):
        patch = ext[4 + c, own, 0:LANES]
        canopy_out[c] = patch
        chosen = exact_dot(by_row, patch)
        for slot in range(2):
            csend[pl.ds(3 * slot + c, gores, stride=8), :] = exact_dot(slots[slot], chosen)
    for slot in range(2):
        csend[pl.ds(6 + slot, gores, stride=8), :] = jnp.broadcast_to(
            jnp.sum(slots[slot], axis=1, keepdims=True), (gores, LANES)
        )
    mine = pl.ds(pl.multiple_of(g * 8, 8), 8)
    crecv[mine, :] = csend[mine, :]
    for i in range(1, gores):
        t = lax.rem(g + i, gores)
        pltpu.make_async_remote_copy(
            csend.at[pl.ds(pl.multiple_of(t * 8, 8), 8)], crecv.at[mine],
            con_sem.at[0], con_sem.at[1], device_id=(s, t), device_id_type=MESH,
        ).start()
    most = pl.ds(0, (gores - 1) * 8)
    pltpu.make_async_copy(crecv.at[most], crecv.at[most], con_sem.at[1]).wait()
    sets_out[...] = crecv[...]

    pltpu.make_async_copy(csend.at[most], csend.at[most], con_sem.at[0]).wait()
    wait_all(outbox, 7, 0)
    wait_all(ansbox, 6, 2)
    for copy in static_halos + moving_halos:
        copy.wait_send()

    def drain(i, carry):
        step, c = lax.div(i, 3), lax.rem(i, 3)
        sent_pair(z_copies(step, c), s, slabs)
        sent_pair(y_copies(step, c), g, gores)
        return carry

    lax.fori_loop(0, 3 * STEPS, drain, 0)
    for c in range(3):
        pltpu.make_async_copy(
            v.at[STEPS, c, pl.ds(1, cz)], fluid_out.at[c], store_sem.at[c]
        ).wait()


def contact_kernel(
    gores, fluid_in, canopy_in, sets, fluid_out, canopy_out, force, xj, fj, acc_ref, pad, field, sem
):
    load = pltpu.make_async_copy(fluid_in, field, sem.at[0])
    store = pltpu.make_async_copy(field, fluid_out, sem.at[1])
    load.start()
    canopy_out[...] = canopy_in[...]
    slots = 2 * gores
    group = 8
    pad[...] = jnp.zeros_like(pad)
    for a in range(slots):
        base = (a // 2) * 8
        flag = sets[base + 6 + a % 2:base + 7 + a % 2, :]
        for c in range(3):
            k = c * slots + a
            row = base + 3 * (a % 2) + c
            point = jnp.where(flag > 0.0, sets[row:row + 1, :], FAR)
            pad[k:k + 1, :] = point
            xj[k] = jnp.broadcast_to(point, (8, LANES))
    points_t = pad[...].T
    pad[...] = points_t
    fj[...] = jnp.zeros_like(fj)

    def block(i, carry):
        at = [pl.ds(pl.multiple_of((i * group + t) * 8, 8), 8) for t in range(group)]
        column = [pad[rows, :] for rows in at]
        for a in range(slots - 2):
            xi = [
                [
                    jnp.broadcast_to(
                        column[t][:, c * slots + a:c * slots + a + 1], (8, LANES)
                    )
                    for c in range(3)
                ]
                for t in range(group)
            ]
            acc = [[None] * 3 for _ in range(group)]
            for b in range(2 * (a // 2) + 2, slots):
                other = [xj[c * slots + b] for c in range(3)]
                pushed = [None] * 3
                for t in range(group):
                    d = [xi[t][c] - other[c] for c in range(3)]
                    square = d[0] * d[0] + d[1] * d[1] + (d[2] * d[2] + SOFTEN)
                    inverse = lax.rsqrt(square)
                    gap = jnp.maximum(REACH - square * inverse, 0.0)
                    weight = gap * gap * inverse
                    for c in range(3):
                        push = weight * d[c]
                        acc[t][c] = push if acc[t][c] is None else acc[t][c] + push
                        pushed[c] = push if pushed[c] is None else pushed[c] + push
                for c in range(3):
                    fj[c * slots + b] = fj[c * slots + b] + pushed[c]
            for t in range(group):
                for c in range(3):
                    acc_ref[c * slots + a, at[t], :] = acc[t][c]

        @pl.when(i == 0)
        def _():
            load.wait()
            store.start()

        return carry

    lax.fori_loop(0, LANES // (8 * group), block, 0)
    for c in range(3):
        for a in range(slots):
            k = c * slots + a
            total = -jnp.sum(fj[k], axis=0, keepdims=True)
            if a < slots - 2:
                total = total + jnp.sum(acc_ref[k].T, axis=0, keepdims=True)
            force[c, a:a + 1, :] = GAIN * total
    store.wait()


def body(
    slabs, gores,
    fluid_velocity, viscosity, pressure_jump, normals, canopy_position, tension,
    slot_cut, couple_dest, couple_block, contact_owner, contact_row,
):
    cz, cy, nx = viscosity.shape
    rows = pressure_jump.shape[0]
    devices = slabs * gores
    zy = cz * cy
    nbx = nx // LANES
    vmem = pl.BlockSpec(memory_space=pltpu.VMEM)
    anywhere = pl.BlockSpec(memory_space=pl.ANY)
    dma = pltpu.SemaphoreType.DMA
    cut_width = min(LANES, slot_cut.shape[0])
    tall = rows + 2 * HALO
    fluid, canopy, sets = pl.pallas_call(
        functools.partial(main_kernel, slabs, gores),
        out_shape=(
            jax.ShapeDtypeStruct(fluid_velocity.shape, F32),
            jax.ShapeDtypeStruct(canopy_position.shape, F32),
            jax.ShapeDtypeStruct((gores * 8, LANES), F32),
        ),
        in_specs=[anywhere] * 11,
        out_specs=(anywhere, vmem, vmem),
        scratch_shapes=[
            pltpu.VMEM(pressure_jump.shape, F32),
            pltpu.VMEM(normals.shape, F32),
            pltpu.VMEM(canopy_position.shape, F32),
            pltpu.VMEM(tension.shape, F32),
            pltpu.VMEM((slot_cut.shape[0] // cut_width, cut_width), jnp.int32),
            pltpu.VMEM((2, rows), jnp.int32),
            pltpu.VMEM((2, rows), jnp.int32),
            pltpu.VMEM(contact_row.shape, jnp.int32),
            pltpu.VMEM(contact_row.shape, jnp.int32),
            pltpu.VMEM((STEPS + 1, 3, cz + 2, cy, nx), F32),
            pltpu.VMEM((cz, cy, nx), F32),
            pltpu.VMEM((STEPS, 2, 3, cz, nx), F32),
            pltpu.VMEM((STEPS, 2, 3, cz, nx), F32),
            pltpu.VMEM((devices * 8, LANES), F32),
            pltpu.VMEM((devices * 8, LANES), F32),
            pltpu.VMEM((devices * 8, LANES), F32),
            pltpu.VMEM((devices * 8, LANES), F32),
            pltpu.VMEM((nbx, zy, 2 * devices), BF16),
            pltpu.VMEM((nbx, 2 * devices, zy), BF16),
            pltpu.VMEM((7, tall, LANES), F32),
            pltpu.VMEM((rows, LANES), F32),
            pltpu.VMEM((rows, LANES), F32),
            pltpu.VMEM((tall, LANES), F32),
            pltpu.VMEM((tall, LANES), F32),
            pltpu.VMEM((3, tall, LANES), F32),
            pltpu.VMEM((rows, LANES), F32),
            pltpu.VMEM((rows, LANES), F32),
            pltpu.VMEM((tall, LANES), F32),
            pltpu.VMEM((tall, LANES), F32),
            pltpu.VMEM((10, tall, 2 * LANES), F32),
            pltpu.VMEM((rows, LANES), F32),
            pltpu.VMEM((gores * 8, LANES), F32),
            pltpu.VMEM((gores * 8, LANES), F32),
            dma((9,)),
            dma((4,)),
            dma((3,)),
            dma((STEPS, 2, 3)),
            dma((STEPS, 2, 3)),
            dma((STEPS, 2, 3)),
            dma((STEPS, 2, 3)),
            dma((4,)),
            dma((16,)),
            dma((16,)),
            dma((2,)),
        ],
        compiler_params=pltpu.CompilerParams(
            collective_id=0, has_side_effects=True, vmem_limit_bytes=56 << 20
        ),
        name="fluid_membrane",
    )(
        fluid_velocity, viscosity, pressure_jump, normals, canopy_position, tension,
        slot_cut.reshape(-1, cut_width),
        couple_dest[0].T, couple_block[0].T, contact_owner[:, :, 0], contact_row,
    )
    slots = 2 * gores
    fluid, canopy, force = pl.pallas_call(
        functools.partial(contact_kernel, gores),
        out_shape=(
            jax.ShapeDtypeStruct(fluid.shape, F32),
            jax.ShapeDtypeStruct(canopy.shape, F32),
            jax.ShapeDtypeStruct((3, slots, LANES), F32),
        ),
        in_specs=[anywhere, vmem, vmem],
        out_specs=(anywhere, vmem, vmem),
        scratch_shapes=[
            pltpu.VMEM((3 * slots, 8, LANES), F32),
            pltpu.VMEM((3 * slots, 8, LANES), F32),
            pltpu.VMEM((3 * slots, LANES, LANES), F32),
            pltpu.VMEM((LANES, LANES), F32),
            pltpu.VMEM(fluid.shape, F32),
            dma((2,)),
        ],
        name="contact",
    )(fluid, canopy, sets)
    return fluid, canopy, jnp.swapaxes(force, 0, 1)[None, None]


def solution(mesh):
    in_specs = (
        P(None, "slab", "gore", None),
        P("slab", "gore", None),
        P("slab", "gore"),
        P(None, "slab", "gore"),
        P(None, "slab", "gore"),
        P(None, "slab", "gore"),
        P(),
        P("gore", "slab", None),
        P("gore", "slab", None),
        P("gore", "slab", None),
        P("gore", "slab"),
    )
    out_specs = (
        P(None, "slab", "gore", None),
        P(None, "slab", "gore"),
        P("slab", "gore", None, None, None),
    )
    step = functools.partial(body, mesh.shape["slab"], mesh.shape["gore"])
    return jax.shard_map(step, mesh=mesh, in_specs=in_specs, out_specs=out_specs, check_vma=False)
```

```python
import functools

import jax
import jax.numpy as jnp
from jax import lax
from jax.experimental import pallas as pl
from jax.experimental.pallas import tpu as pltpu
from jax.sharding import PartitionSpec as P

STEPS = 3
SWEEPS = 8
HALO = 8
LANES = 128
GAIN = 0.1
REACH = 1.0
SOFTEN = 0.01
FAR = 1.0e15
MESH = pl.DeviceIdType.MESH
F32 = jnp.float32
BF16 = jnp.bfloat16


def iota(shape, dim):
    return lax.broadcasted_iota(jnp.int32, shape, dim)


def dot(a, b):
    return lax.dot_general(a, b, (((1,), (0,)), ((), ())), preferred_element_type=F32)


def exact_dot(a, b):
    return lax.dot_general(
        a, b, (((1,), (0,)), ((), ())),
        precision=lax.Precision.HIGHEST, preferred_element_type=F32,
    )


def split(x):
    hi = x.astype(BF16)
    return hi, (x - hi.astype(F32)).astype(BF16)


def to_column(row):
    n = row.shape[1]
    same = iota((n, n), 0) == iota((n, n), 1)
    return jnp.sum(jnp.where(same, jnp.broadcast_to(row, (n, n)), 0.0), axis=1, keepdims=True)


def main_kernel(
    slabs, gores,
    fluid_hbm, visc_hbm, jump_hbm, normals_hbm, canopy_hbm, tension_hbm, cut_hbm,
    dest_hbm, block_hbm, owner_hbm, picked_hbm,
    fluid_out, canopy_out, sets_out,
    jump, normals, canopy, tension, cut, dest, block, owner, picked,
    v, vis, yh, ys, outbox, inbox, ansbox, retbox, hot_t, hot,
    sc, spr, spl, sl, sr, dc, dpr, dpl, dl, dr, ext, inv, csend, crecv,
    small_sem, load_sem, zs_sem, zr_sem, ysend_sem, yr_sem, a2a_sem, mem_s, mem_r, con_sem,
):
    s = lax.axis_index("slab")
    g = lax.axis_index("gore")
    me = s * gores + g
    devices = slabs * gores
    cz, cy, nx = vis.shape
    zy = cz * cy
    nbx = nx // LANES
    rows = jump.shape[0]

    def device(t):
        return (lax.div(t, gores), lax.rem(t, gores))

    def rows_of(t, count):
        return pl.ds(pl.multiple_of(t * 8, 8), count)

    loads = [
        pltpu.make_async_copy(fluid_hbm.at[c], v.at[0, c, pl.ds(1, cz)], load_sem.at[c])
        for c in range(3)
    ]
    loads.append(pltpu.make_async_copy(visc_hbm, vis, load_sem.at[3]))
    small = [
        pltpu.make_async_copy(src, dst, small_sem.at[i])
        for i, (src, dst) in enumerate((
            (dest_hbm, dest), (block_hbm, block), (jump_hbm, jump), (normals_hbm, normals),
            (canopy_hbm, canopy), (tension_hbm, tension), (cut_hbm, cut),
            (owner_hbm, owner), (picked_hbm, picked),
        ))
    ]
    for copy in small + loads:
        copy.start()
    barrier = pltpu.get_barrier_semaphore()

    def greet(i, carry):
        t = lax.rem(me + i, devices)
        pl.semaphore_signal(barrier, inc=1, device_id=device(t), device_id_type=MESH)
        return carry

    lax.fori_loop(1, devices, greet, 0)

    for copy in small:
        copy.wait()

    dest_row = jnp.concatenate([dest[0:1, :], dest[1:2, :]], axis=1).astype(F32)
    line_row = jnp.concatenate([block[0:1, :], block[1:2, :]], axis=1).astype(F32)
    entries = 2 * rows
    dest_col = to_column(dest_row)
    line_col = to_column(line_row) + 1.0
    by_dev = (iota((devices, entries), 0).astype(F32) == dest_row).astype(F32)
    by_entry = (iota((entries, devices), 1).astype(F32) == dest_col).astype(F32)
    row_a = lax.rem(iota((entries, entries), 0), rows)
    row_b = lax.rem(iota((entries, entries), 1), rows)
    rank_dev = dot(by_dev.astype(BF16), (row_a < row_b).astype(BF16))
    rank_entry = dot((row_b < row_a).astype(BF16), by_entry.astype(BF16))
    surface = [jump[...] * normals[c] * 0.25 for c in range(3)]
    columns = [jnp.concatenate([t, t], axis=0) for t in surface]
    columns.append(jnp.broadcast_to(line_col, (entries, LANES)))
    table = jnp.concatenate(columns, axis=1)
    table_hi, table_lo = split(table)
    pick = jnp.concatenate(
        [jnp.where(rank_dev == float(slot), by_dev, 0.0) for slot in range(2)], axis=0
    ).astype(BF16)
    placed = dot(pick, table_hi) + dot(pick, table_lo)
    for slot in range(2):
        for c in range(3):
            outbox[pl.ds(3 * slot + c, devices, stride=8), :] = (
                placed[slot * devices:(slot + 1) * devices, c * LANES:(c + 1) * LANES]
            )
    outbox[pl.ds(6, devices, stride=8), :] = jnp.where(
        iota((devices, LANES), 1) < LANES // 2,
        placed[:devices, 3 * LANES:], placed[devices:, 3 * LANES:],
    )
    back_pick = jnp.concatenate(
        [jnp.where(rank_entry == float(slot), by_entry, 0.0) for slot in range(2)], axis=1
    ).astype(BF16)

    pl.semaphore_wait(barrier, devices - 1)
    inbox[rows_of(me, 8), :] = outbox[rows_of(me, 8), :]

    def send_all(source, target, count, sem):
        def one(i, carry):
            t = lax.rem(me + i, devices)
            pltpu.make_async_remote_copy(
                source.at[rows_of(t, count)], target.at[rows_of(me, count)],
                a2a_sem.at[sem], a2a_sem.at[sem + 1],
                device_id=device(t), device_id_type=MESH,
            ).start()
            return carry

        lax.fori_loop(1, devices, one, 0)

    def wait_all(buffer, count, sem):
        part = buffer.at[pl.ds(0, (devices - 1) * count)]
        pltpu.make_async_copy(part, part, a2a_sem.at[sem]).wait()

    send_all(outbox, inbox, 7, 0)

    zero_plane = jnp.zeros((cy, nx), F32)
    zero_edge = jnp.zeros((cz, nx), F32)

    @pl.when(s == 0)
    def _():
        for step in range(STEPS):
            for c in range(3):
                v[step, c, 0] = zero_plane

    @pl.when(s == slabs - 1)
    def _():
        for step in range(STEPS):
            for c in range(3):
                v[step, c, cz + 1] = zero_plane

    @pl.when(g == 0)
    def _():
        for step in range(STEPS):
            for c in range(3):
                yh[step, 0, c] = zero_edge

    @pl.when(g == gores - 1)
    def _():
        for step in range(STEPS):
            for c in range(3):
                yh[step, 1, c] = zero_edge

    first = s * rows
    cut_f = cut[...].astype(F32)
    cut_rows, cut_width = cut.shape
    node = first + iota((rows, cut_width), 0)
    lane = iota((rows, cut_width), 1)
    down = jnp.zeros((rows, cut_width), F32)
    up = jnp.zeros((rows, cut_width), F32)
    total_rows = slabs * rows
    for q in range(cut_rows):
        index = q * cut_width + lane
        keep = jnp.broadcast_to(1.0 - cut_f[q:q + 1, :], (rows, cut_width))
        down += jnp.where((index == node) & (index < total_rows - 1), keep, 0.0)
        up += jnp.where(index == node - 1, keep, 0.0)
    keep_down = jnp.sum(down, axis=1, keepdims=True)
    keep_up = jnp.sum(up, axis=1, keepdims=True)
    w_up = tension[0] * keep_up
    w_down = tension[1] * keep_down
    w_left = tension[2]
    w_right = tension[3]
    scale = 1.0 / (1.0 + w_up + w_down + w_left + w_right)
    inv[...] = scale
    own = pl.ds(HALO, rows)
    for i, w in enumerate((w_up, w_down, w_left, w_right)):
        sc[i, own, :] = w * scale
    for c in range(3):
        sc[4 + c, own, :] = canopy[c]

    wait_all(inbox, 7, 1)

    def z_copies(step, c):
        up_copy = pltpu.make_async_remote_copy(
            v.at[step, c, cz], v.at[step, c, 0], zs_sem.at[step, 0, c], zr_sem.at[step, 0, c],
            device_id=(lax.rem(s + 1, slabs), g), device_id_type=MESH,
        )
        down_copy = pltpu.make_async_remote_copy(
            v.at[step, c, 1], v.at[step, c, cz + 1], zs_sem.at[step, 1, c], zr_sem.at[step, 1, c],
            device_id=(lax.rem(s + slabs - 1, slabs), g), device_id_type=MESH,
        )
        return up_copy, down_copy

    def y_copies(step, c):
        up_copy = pltpu.make_async_remote_copy(
            ys.at[step, 0, c], yh.at[step, 0, c], ysend_sem.at[step, 0, c], yr_sem.at[step, 0, c],
            device_id=(s, lax.rem(g + 1, gores)), device_id_type=MESH,
        )
        down_copy = pltpu.make_async_remote_copy(
            ys.at[step, 1, c], yh.at[step, 1, c], ysend_sem.at[step, 1, c], yr_sem.at[step, 1, c],
            device_id=(s, lax.rem(g + gores - 1, gores)), device_id_type=MESH,
        )
        return up_copy, down_copy

    def start_pair(pair, at, length):
        @pl.when(at < length - 1)
        def _():
            pair[0].start()

        @pl.when(at > 0)
        def _():
            pair[1].start()

    def recv_pair(pair, at, length):
        @pl.when(at > 0)
        def _():
            pair[0].wait_recv()

        @pl.when(at < length - 1)
        def _():
            pair[1].wait_recv()

    def sent_pair(pair, at, length):
        @pl.when(at < length - 1)
        def _():
            pair[0].wait_send()

        @pl.when(at > 0)
        def _():
            pair[1].wait_send()

    meta = inbox[pl.ds(6, devices, stride=8), :]
    meta_t = meta.T
    line_t = jnp.concatenate(
        [meta_t[0:1, :], meta_t[LANES // 2:LANES // 2 + 1, :]], axis=1
    )
    parts = []
    for c in range(3):
        tiles = jnp.concatenate(
            [inbox[pl.ds(3 * slot + c, devices, stride=8), :] for slot in range(2)], axis=0
        )
        parts.append(jnp.concatenate(split(tiles), axis=1))
    first_line = (iota((zy, 2 * devices), 0) * nbx + 1).astype(F32)
    for c in range(3):
        loads[c].wait()
        for x in range(nbx):
            if c == 0:
                hot_t[x] = jnp.where(line_t == first_line + float(x), 1.0, 0.0).astype(BF16)
            matrix = hot_t[x]
            added = dot(matrix, parts[c])
            added = added[:, :LANES] + added[:, LANES:]
            cols = pl.ds(x * LANES, LANES)
            here = v[0, c, pl.ds(1, cz), :, cols]
            v[0, c, pl.ds(1, cz), :, cols] = here + added.reshape(cz, cy, LANES)
        start_pair(z_copies(0, c), s, slabs)
        for z in range(cz):
            ys[0, 0, c, z:z + 1, :] = v[0, c, z + 1, cy - 1:cy, :]
            ys[0, 1, c, z:z + 1, :] = v[0, c, z + 1, 0:1, :]
        start_pair(y_copies(0, c), g, gores)
    loads[3].wait()

    def neighbours(mid, to_right, to_left, left, right, base):
        below, above = lax.rem(s + 1, slabs), lax.rem(s + slabs - 1, slabs)
        after, before = lax.rem(g + 1, gores), lax.rem(g + gores - 1, gores)
        over, under = pl.ds(0, HALO), pl.ds(rows + HALO, HALO)
        head, tail = pl.ds(0, HALO), pl.ds(rows - HALO, HALO)
        plan = (
            (to_right, left.at[own], (s, after)),
            (to_left, right.at[own], (s, before)),
            (mid.at[:, pl.ds(rows, HALO)], mid.at[:, over], (below, g)),
            (mid.at[:, pl.ds(HALO, HALO)], mid.at[:, under], (above, g)),
            (to_right.at[tail], left.at[over], (below, after)),
            (to_left.at[tail], right.at[over], (below, before)),
            (to_right.at[head], left.at[under], (above, after)),
            (to_left.at[head], right.at[under], (above, before)),
        )
        return [
            pltpu.make_async_remote_copy(
                src, to, mem_s.at[base + i], mem_r.at[base + i],
                device_id=where, device_id_type=MESH,
            )
            for i, (src, to, where) in enumerate(plan)
        ]

    band = lax.div(iota((rows, LANES), 1), HALO)

    def pack(mid, to_right, to_left, count):
        going_right = jnp.zeros((rows, LANES), F32)
        going_left = jnp.zeros((rows, LANES), F32)
        for i in range(count):
            part = mid[i, own, :]
            going_right = jnp.where(
                band == i, pltpu.roll(part, HALO * (i + 1), 1), going_right
            )
            moved = part if i == 0 else pltpu.roll(part, HALO * i, 1)
            going_left = jnp.where(band == i, moved, going_left)
        to_right[...] = going_right
        to_left[...] = going_left

    wide = iota((rows + 2 * HALO, LANES), 1)

    def unpack(mid, left, right, i):
        from_left = pltpu.roll(left[...], LANES - HALO * (i + 1), 1)
        from_right = right[...] if i == 0 else pltpu.roll(right[...], LANES - HALO * i, 1)
        side = jnp.where(wide < HALO, from_right, 0.0)
        side = jnp.where(wide >= LANES - HALO, from_left, side)
        return mid[i], side

    pack(sc, spr, spl, 7)
    static_halos = neighbours(sc, spr, spl, sl, sr, 0)

    at_line = (iota((devices, zy), 1) * nbx + 1).astype(F32)
    for slot in range(2):
        named = jnp.broadcast_to(
            meta[:, slot * (LANES // 2):slot * (LANES // 2) + 1], (devices, zy)
        )
        for x in range(nbx):
            hot[x, slot * devices:(slot + 1) * devices, :] = jnp.where(
                named == at_line + float(x), 1.0, 0.0
            ).astype(BF16)

    sub = iota((8, nx), 0)
    lan = iota((8, nx), 1)

    def plane(step, c, z, stage):
        blocks = cy // 8
        center = v[step, c, z + 1, pl.ds(0, 8), :]
        up_roll = jnp.broadcast_to(yh[step, 0, c, pl.ds(z, 1), :], (8, nx))
        down_roll = pltpu.roll(center, 7, 0)
        for yb in range(blocks):
            at = pl.ds(8 * yb, 8)
            rolled = pltpu.roll(center, 1, 0)
            upper = jnp.where(sub == 0, up_roll, rolled)
            if yb + 1 < blocks:
                following = v[step, c, z + 1, pl.ds(8 * yb + 8, 8), :]
                next_roll = pltpu.roll(following, 7, 0)
            else:
                following = None
                next_roll = jnp.broadcast_to(yh[step, 1, c, pl.ds(z, 1), :], (8, nx))
            lower = jnp.where(sub == 7, next_roll, down_roll)
            total = v[step, c, z, at, :] + v[step, c, z + 2, at, :]
            total = total + upper + lower
            total = total + jnp.where(lan == 0, 0.0, pltpu.roll(center, 1, 1))
            total = total + jnp.where(lan == nx - 1, 0.0, pltpu.roll(center, nx - 1, 1))
            new = center + vis[z, at, :] * (total - 6.0 * center)
            if stage:
                v[step + 1, c, z + 1, at, :] = new
            else:
                fluid_out[c, z, at, :] = new
            if stage and yb == 0:
                ys[step + 1, 1, c, pl.ds(z, 1), :] = new[0:1, :]
            if stage and yb == blocks - 1:
                ys[step + 1, 0, c, pl.ds(z, 1), :] = new[7:8, :]
            center, up_roll, down_roll = following, rolled, next_roll

    def substep(step, c, stage):
        recv_pair(y_copies(step, c), g, gores)

        def inner(z, carry):
            plane(step, c, z, stage)
            return carry

        lax.fori_loop(1, cz - 1, inner, 0)
        recv_pair(z_copies(step, c), s, slabs)
        plane(step, c, 0, stage)
        plane(step, c, cz - 1, stage)
        if stage:
            start_pair(z_copies(step + 1, c), s, slabs)
            start_pair(y_copies(step + 1, c), g, gores)

    def early(i, carry):
        substep(lax.div(i, 3), lax.rem(i, 3), True)
        return carry

    lax.fori_loop(0, 3 * (STEPS - 1), early, 0)
    for copy in static_halos:
        copy.start()

    def last(c, carry):
        substep(STEPS - 1, c, False)
        sampled = jnp.zeros((2 * devices, 2 * LANES), F32)
        for x in range(nbx):
            cell = fluid_out[c, :, :, pl.ds(x * LANES, LANES)].reshape(zy, LANES)
            sampled = sampled + dot(hot[x], jnp.concatenate(split(cell), axis=1))
        sampled = sampled[:, :LANES] + sampled[:, LANES:]
        for slot in range(2):
            ansbox[pl.ds(3 * slot + c, devices, stride=8), :] = (
                sampled[slot * devices:(slot + 1) * devices]
            )
        return carry

    lax.fori_loop(0, 3, last, 0)

    retbox[rows_of(me, 8), :] = ansbox[rows_of(me, 8), :]
    send_all(ansbox, retbox, 6, 2)
    wait_all(retbox, 6, 3)
    for c in range(3):
        hi, lo = split(
            jnp.concatenate(
                [retbox[pl.ds(3 * slot + c, devices, stride=8), :] for slot in range(2)], axis=0
            )
        )
        taken = dot(back_pick, hi) + dot(back_pick, lo)
        node_velocity = (taken[:rows] + taken[rows:]) * 0.5
        dc[c, own, :] = (canopy[c] + node_velocity) * inv[...]

    pack(dc, dpr, dpl, 3)
    moving_halos = neighbours(dc, dpr, dpl, dl, dr, 8)
    for copy in moving_halos:
        copy.start()

    for copy in static_halos:
        copy.wait_recv()
    for i in range(7):
        middle, side = unpack(sc, sl, sr, i)
        ext[i, :, 0:LANES] = middle
        ext[i, :, LANES:2 * LANES] = side
    for copy in moving_halos:
        copy.wait_recv()
    for c in range(3):
        middle, side = unpack(dc, dl, dr, c)
        ext[7 + c, :, 0:LANES] = middle
        ext[7 + c, :, LANES:2 * LANES] = side

    height = rows + 2 * HALO

    def sweep(i, carry):
        for c in range(3):
            p = ext[4 + c]
            new = ext[7 + c] + ext[0] * pltpu.roll(p, 1, 0)
            new = new + ext[1] * pltpu.roll(p, height - 1, 0)
            new = new + ext[2] * pltpu.roll(p, 1, 1)
            new = new + ext[3] * pltpu.roll(p, 2 * LANES - 1, 1)
            ext[4 + c] = new
        return carry

    lax.fori_loop(0, SWEEPS, sweep, 0)

    listed = owner.shape[1]
    owner_f = owner[...].astype(F32)
    picked_col = to_column(picked[...].astype(F32))
    by_owner = (iota((gores, listed), 0).astype(F32) == owner_f).astype(F32)
    before = (iota((listed, listed), 0) < iota((listed, listed), 1)).astype(F32)
    rank = exact_dot(by_owner, before)
    by_row = (iota((listed, rows), 1).astype(F32) == picked_col).astype(F32)
    slots = [jnp.where(rank == float(slot), by_owner, 0.0) for slot in range(2)]
    for c in range(3):
        patch = ext[4 + c, own, 0:LANES]
        canopy_out[c] = patch
        chosen = exact_dot(by_row, patch)
        for slot in range(2):
            csend[pl.ds(3 * slot + c, gores, stride=8), :] = exact_dot(slots[slot], chosen)
    for slot in range(2):
        csend[pl.ds(6 + slot, gores, stride=8), :] = jnp.broadcast_to(
            jnp.sum(slots[slot], axis=1, keepdims=True), (gores, LANES)
        )
    mine = pl.ds(pl.multiple_of(g * 8, 8), 8)
    crecv[mine, :] = csend[mine, :]
    for i in range(1, gores):
        t = lax.rem(g + i, gores)
        pltpu.make_async_remote_copy(
            csend.at[pl.ds(pl.multiple_of(t * 8, 8), 8)], crecv.at[mine],
            con_sem.at[0], con_sem.at[1], device_id=(s, t), device_id_type=MESH,
        ).start()
    most = pl.ds(0, (gores - 1) * 8)
    pltpu.make_async_copy(crecv.at[most], crecv.at[most], con_sem.at[1]).wait()
    sets_out[...] = crecv[...]

    pltpu.make_async_copy(csend.at[most], csend.at[most], con_sem.at[0]).wait()
    wait_all(outbox, 7, 0)
    wait_all(ansbox, 6, 2)
    for copy in static_halos + moving_halos:
        copy.wait_send()

    def drain(i, carry):
        step, c = lax.div(i, 3), lax.rem(i, 3)
        sent_pair(z_copies(step, c), s, slabs)
        sent_pair(y_copies(step, c), g, gores)
        return carry

    lax.fori_loop(0, 3 * STEPS, drain, 0)


def contact_kernel(
    gores, fluid_in, canopy_in, sets, fluid_out, canopy_out, force, xj, fj, acc_ref, pad, sem
):
    stores = (
        pltpu.make_async_copy(fluid_in, fluid_out, sem.at[0]),
        pltpu.make_async_copy(canopy_in, canopy_out, sem.at[1]),
    )
    for store in stores:
        store.start()
    slots = 2 * gores
    group = 8
    pad[...] = jnp.zeros_like(pad)
    for a in range(slots):
        base = (a // 2) * 8
        flag = sets[base + 6 + a % 2:base + 7 + a % 2, :]
        for c in range(3):
            k = c * slots + a
            row = base + 3 * (a % 2) + c
            point = jnp.where(flag > 0.0, sets[row:row + 1, :], FAR)
            pad[k:k + 1, :] = point
            xj[k] = jnp.broadcast_to(point, (8, LANES))
    points_t = pad[...].T
    pad[...] = points_t
    fj[...] = jnp.zeros_like(fj)

    def block(i, carry):
        at = [pl.ds(pl.multiple_of((i * group + t) * 8, 8), 8) for t in range(group)]
        column = [pad[rows, :] for rows in at]
        for a in range(slots - 2):
            xi = [
                [
                    jnp.broadcast_to(
                        column[t][:, c * slots + a:c * slots + a + 1], (8, LANES)
                    )
                    for c in range(3)
                ]
                for t in range(group)
            ]
            acc = [[None] * 3 for _ in range(group)]
            for b in range(2 * (a // 2) + 2, slots):
                other = [xj[c * slots + b] for c in range(3)]
                pushed = [None] * 3
                for t in range(group):
                    d = [xi[t][c] - other[c] for c in range(3)]
                    square = d[0] * d[0] + d[1] * d[1] + (d[2] * d[2] + SOFTEN)
                    inverse = lax.rsqrt(square)
                    gap = jnp.maximum(REACH - square * inverse, 0.0)
                    weight = gap * gap * inverse
                    for c in range(3):
                        push = weight * d[c]
                        acc[t][c] = push if acc[t][c] is None else acc[t][c] + push
                        pushed[c] = push if pushed[c] is None else pushed[c] + push
                for c in range(3):
                    fj[c * slots + b] = fj[c * slots + b] + pushed[c]
            for t in range(group):
                for c in range(3):
                    acc_ref[c * slots + a, at[t], :] = acc[t][c]
        return carry

    lax.fori_loop(0, LANES // (8 * group), block, 0)
    for c in range(3):
        for a in range(slots):
            k = c * slots + a
            total = -jnp.sum(fj[k], axis=0, keepdims=True)
            if a < slots - 2:
                total = total + jnp.sum(acc_ref[k].T, axis=0, keepdims=True)
            force[c, a:a + 1, :] = GAIN * total
    for store in stores:
        store.wait()


def body(
    slabs, gores,
    fluid_velocity, viscosity, pressure_jump, normals, canopy_position, tension,
    slot_cut, couple_dest, couple_block, contact_owner, contact_row,
):
    cz, cy, nx = viscosity.shape
    rows = pressure_jump.shape[0]
    devices = slabs * gores
    zy = cz * cy
    nbx = nx // LANES
    vmem = pl.BlockSpec(memory_space=pltpu.VMEM)
    anywhere = pl.BlockSpec(memory_space=pl.ANY)
    dma = pltpu.SemaphoreType.DMA
    cut_width = min(LANES, slot_cut.shape[0])
    tall = rows + 2 * HALO
    fluid, canopy, sets = pl.pallas_call(
        functools.partial(main_kernel, slabs, gores),
        out_shape=(
            jax.ShapeDtypeStruct(fluid_velocity.shape, F32),
            jax.ShapeDtypeStruct(canopy_position.shape, F32),
            jax.ShapeDtypeStruct((gores * 8, LANES), F32),
        ),
        in_specs=[pl.BlockSpec(memory_space=pltpu.HBM)] * 11,
        out_specs=(vmem, vmem, vmem),
        scratch_shapes=[
            pltpu.VMEM(pressure_jump.shape, F32),
            pltpu.VMEM(normals.shape, F32),
            pltpu.VMEM(canopy_position.shape, F32),
            pltpu.VMEM(tension.shape, F32),
            pltpu.VMEM((slot_cut.shape[0] // cut_width, cut_width), jnp.int32),
            pltpu.VMEM((2, rows), jnp.int32),
            pltpu.VMEM((2, rows), jnp.int32),
            pltpu.VMEM(contact_row.shape, jnp.int32),
            pltpu.VMEM(contact_row.shape, jnp.int32),
            pltpu.VMEM((STEPS, 3, cz + 2, cy, nx), F32),
            pltpu.VMEM((cz, cy, nx), F32),
            pltpu.VMEM((STEPS, 2, 3, cz, nx), F32),
            pltpu.VMEM((STEPS, 2, 3, cz, nx), F32),
            pltpu.VMEM((devices * 8, LANES), F32),
            pltpu.VMEM((devices * 8, LANES), F32),
            pltpu.VMEM((devices * 8, LANES), F32),
            pltpu.VMEM((devices * 8, LANES), F32),
            pltpu.VMEM((nbx, zy, 2 * devices), BF16),
            pltpu.VMEM((nbx, 2 * devices, zy), BF16),
            pltpu.VMEM((7, tall, LANES), F32),
            pltpu.VMEM((rows, LANES), F32),
            pltpu.VMEM((rows, LANES), F32),
            pltpu.VMEM((tall, LANES), F32),
            pltpu.VMEM((tall, LANES), F32),
            pltpu.VMEM((3, tall, LANES), F32),
            pltpu.VMEM((rows, LANES), F32),
            pltpu.VMEM((rows, LANES), F32),
            pltpu.VMEM((tall, LANES), F32),
            pltpu.VMEM((tall, LANES), F32),
            pltpu.VMEM((10, tall, 2 * LANES), F32),
            pltpu.VMEM((rows, LANES), F32),
            pltpu.VMEM((gores * 8, LANES), F32),
            pltpu.VMEM((gores * 8, LANES), F32),
            dma((9,)),
            dma((4,)),
            dma((STEPS, 2, 3)),
            dma((STEPS, 2, 3)),
            dma((STEPS, 2, 3)),
            dma((STEPS, 2, 3)),
            dma((4,)),
            dma((16,)),
            dma((16,)),
            dma((2,)),
        ],
        compiler_params=pltpu.CompilerParams(
            collective_id=0, has_side_effects=True, vmem_limit_bytes=26 << 20
        ),
        name="fluid_membrane",
    )(*(
        pltpu.with_memory_space_constraint(x, pltpu.HBM)
        for x in (
            fluid_velocity, viscosity, pressure_jump, normals, canopy_position, tension,
            slot_cut.reshape(-1, cut_width),
            couple_dest[0].T, couple_block[0].T, contact_owner[:, :, 0], contact_row,
        )
    ))
    slots = 2 * gores
    fluid, canopy, force = pl.pallas_call(
        functools.partial(contact_kernel, gores),
        out_shape=(
            jax.ShapeDtypeStruct(fluid.shape, F32),
            jax.ShapeDtypeStruct(canopy.shape, F32),
            jax.ShapeDtypeStruct((3, slots, LANES), F32),
        ),
        in_specs=[vmem, vmem, vmem],
        out_specs=(anywhere, anywhere, vmem),
        scratch_shapes=[
            pltpu.VMEM((3 * slots, 8, LANES), F32),
            pltpu.VMEM((3 * slots, 8, LANES), F32),
            pltpu.VMEM((3 * slots, LANES, LANES), F32),
            pltpu.VMEM((LANES, LANES), F32),
            dma((2,)),
        ],
        compiler_params=pltpu.CompilerParams(vmem_limit_bytes=12 << 20),
        name="contact",
    )(fluid, canopy, sets)
    return fluid, canopy, jnp.swapaxes(force, 0, 1)[None, None]


def solution(mesh):
    in_specs = (
        P(None, "slab", "gore", None),
        P("slab", "gore", None),
        P("slab", "gore"),
        P(None, "slab", "gore"),
        P(None, "slab", "gore"),
        P(None, "slab", "gore"),
        P(),
        P("gore", "slab", None),
        P("gore", "slab", None),
        P("gore", "slab", None),
        P("gore", "slab"),
    )
    out_specs = (
        P(None, "slab", "gore", None),
        P(None, "slab", "gore"),
        P("slab", "gore", None, None, None),
    )
    step = functools.partial(body, mesh.shape["slab"], mesh.shape["gore"])
    return jax.shard_map(step, mesh=mesh, in_specs=in_specs, out_specs=out_specs, check_vma=False)
```

```python
import functools

import jax
import jax.numpy as jnp
from jax import lax
from jax.experimental import pallas as pl
from jax.experimental.pallas import tpu as pltpu
from jax.sharding import PartitionSpec as P

STEPS = 3
SWEEPS = 8
HALO = 8
LANES = 128
GAIN = 0.1
REACH = 1.0
SOFTEN = 0.01
FAR = 1.0e15
MESH = pl.DeviceIdType.MESH
F32 = jnp.float32
BF16 = jnp.bfloat16


def iota(shape, dim):
    return lax.broadcasted_iota(jnp.int32, shape, dim)


def dot(a, b):
    return lax.dot_general(a, b, (((1,), (0,)), ((), ())), preferred_element_type=F32)


def exact_dot(a, b):
    return lax.dot_general(
        a, b, (((1,), (0,)), ((), ())),
        precision=lax.Precision.HIGHEST, preferred_element_type=F32,
    )


def split(x):
    hi = x.astype(BF16)
    return hi, (x - hi.astype(F32)).astype(BF16)


def to_column(row):
    n = row.shape[1]
    same = iota((n, n), 0) == iota((n, n), 1)
    return jnp.sum(jnp.where(same, jnp.broadcast_to(row, (n, n)), 0.0), axis=1, keepdims=True)


def main_kernel(
    slabs, gores,
    fluid_hbm, visc_hbm, jump_hbm, normals_hbm, canopy_hbm, tension_hbm, cut_hbm,
    dest_hbm, block_hbm, owner_hbm, picked_hbm,
    fluid_out, canopy_out, sets_out,
    jump, normals, canopy, tension, cut, dest, block, owner, picked,
    v, vis, yh, ys, outbox, inbox, ansbox, retbox, hot_t, hot,
    sc, spr, spl, sl, sr, dc, dpr, dpl, dl, dr, ext, inv, csend, crecv,
    small_sem, load_sem, zs_sem, zr_sem, ysend_sem, yr_sem, a2a_sem, mem_s, mem_r, con_sem,
):
    s = lax.axis_index("slab")
    g = lax.axis_index("gore")
    me = s * gores + g
    devices = slabs * gores
    cz, cy, nx = vis.shape
    zy = cz * cy
    nbx = nx // LANES
    rows = jump.shape[0]

    def device(t):
        return (lax.div(t, gores), lax.rem(t, gores))

    def rows_of(t, count):
        return pl.ds(pl.multiple_of(t * 8, 8), count)

    loads = [
        pltpu.make_async_copy(fluid_hbm.at[c], v.at[0, c, pl.ds(1, cz)], load_sem.at[c])
        for c in range(3)
    ]
    loads.append(pltpu.make_async_copy(visc_hbm, vis, load_sem.at[3]))
    small = [
        pltpu.make_async_copy(src, dst, small_sem.at[i])
        for i, (src, dst) in enumerate((
            (dest_hbm, dest), (block_hbm, block), (jump_hbm, jump), (normals_hbm, normals),
            (canopy_hbm, canopy), (tension_hbm, tension), (cut_hbm, cut),
            (owner_hbm, owner), (picked_hbm, picked),
        ))
    ]
    for copy in small + loads:
        copy.start()
    barrier = pltpu.get_barrier_semaphore()

    def greet(i, carry):
        t = lax.rem(me + i, devices)
        pl.semaphore_signal(barrier, inc=1, device_id=device(t), device_id_type=MESH)
        return carry

    lax.fori_loop(1, devices, greet, 0)

    for copy in small:
        copy.wait()

    dest_row = jnp.concatenate([dest[0:1, :], dest[1:2, :]], axis=1).astype(F32)
    line_row = jnp.concatenate([block[0:1, :], block[1:2, :]], axis=1).astype(F32)
    entries = 2 * rows
    dest_col = to_column(dest_row)
    line_col = to_column(line_row) + 1.0
    by_dev = (iota((devices, entries), 0).astype(F32) == dest_row).astype(F32)
    by_entry = (iota((entries, devices), 1).astype(F32) == dest_col).astype(F32)
    row_a = lax.rem(iota((entries, entries), 0), rows)
    row_b = lax.rem(iota((entries, entries), 1), rows)
    rank_dev = dot(by_dev.astype(BF16), (row_a < row_b).astype(BF16))
    rank_entry = dot((row_b < row_a).astype(BF16), by_entry.astype(BF16))
    surface = [jump[...] * normals[c] * 0.25 for c in range(3)]
    columns = [jnp.concatenate([t, t], axis=0) for t in surface]
    columns.append(jnp.broadcast_to(line_col, (entries, LANES)))
    table = jnp.concatenate(columns, axis=1)
    table_hi, table_lo = split(table)
    pick = jnp.concatenate(
        [jnp.where(rank_dev == float(slot), by_dev, 0.0) for slot in range(2)], axis=0
    ).astype(BF16)
    placed = dot(pick, table_hi) + dot(pick, table_lo)
    for slot in range(2):
        for c in range(3):
            outbox[pl.ds(3 * slot + c, devices, stride=8), :] = (
                placed[slot * devices:(slot + 1) * devices, c * LANES:(c + 1) * LANES]
            )
    outbox[pl.ds(6, devices, stride=8), :] = jnp.where(
        iota((devices, LANES), 1) < LANES // 2,
        placed[:devices, 3 * LANES:], placed[devices:, 3 * LANES:],
    )
    back_pick = jnp.concatenate(
        [jnp.where(rank_entry == float(slot), by_entry, 0.0) for slot in range(2)], axis=1
    ).astype(BF16)

    pl.semaphore_wait(barrier, devices - 1)
    inbox[rows_of(me, 8), :] = outbox[rows_of(me, 8), :]

    def send_all(source, target, count, sem):
        def one(i, carry):
            t = lax.rem(me + i, devices)
            pltpu.make_async_remote_copy(
                source.at[rows_of(t, count)], target.at[rows_of(me, count)],
                a2a_sem.at[sem], a2a_sem.at[sem + 1],
                device_id=device(t), device_id_type=MESH,
            ).start()
            return carry

        lax.fori_loop(1, devices, one, 0)

    def wait_all(buffer, count, sem):
        part = buffer.at[pl.ds(0, (devices - 1) * count)]
        pltpu.make_async_copy(part, part, a2a_sem.at[sem]).wait()

    send_all(outbox, inbox, 7, 0)

    zero_plane = jnp.zeros((cy, nx), F32)
    zero_edge = jnp.zeros((cz, nx), F32)

    @pl.when(s == 0)
    def _():
        for step in range(STEPS):
            for c in range(3):
                v[step, c, 0] = zero_plane

    @pl.when(s == slabs - 1)
    def _():
        for step in range(STEPS):
            for c in range(3):
                v[step, c, cz + 1] = zero_plane

    @pl.when(g == 0)
    def _():
        for step in range(STEPS):
            for c in range(3):
                yh[step, 0, c] = zero_edge

    @pl.when(g == gores - 1)
    def _():
        for step in range(STEPS):
            for c in range(3):
                yh[step, 1, c] = zero_edge

    first = s * rows
    cut_f = cut[...].astype(F32)
    cut_rows, cut_width = cut.shape
    node = first + iota((rows, cut_width), 0)
    lane = iota((rows, cut_width), 1)
    down = jnp.zeros((rows, cut_width), F32)
    up = jnp.zeros((rows, cut_width), F32)
    total_rows = slabs * rows
    for q in range(cut_rows):
        index = q * cut_width + lane
        keep = jnp.broadcast_to(1.0 - cut_f[q:q + 1, :], (rows, cut_width))
        down += jnp.where((index == node) & (index < total_rows - 1), keep, 0.0)
        up += jnp.where(index == node - 1, keep, 0.0)
    keep_down = jnp.sum(down, axis=1, keepdims=True)
    keep_up = jnp.sum(up, axis=1, keepdims=True)
    w_up = tension[0] * keep_up
    w_down = tension[1] * keep_down
    w_left = tension[2]
    w_right = tension[3]
    scale = 1.0 / (1.0 + w_up + w_down + w_left + w_right)
    inv[...] = scale
    own = pl.ds(HALO, rows)
    for i, w in enumerate((w_up, w_down, w_left, w_right)):
        sc[i, own, :] = w * scale
    for c in range(3):
        sc[4 + c, own, :] = canopy[c]

    listed = owner.shape[1]
    owner_f = owner[...].astype(F32)
    picked_col = to_column(picked[...].astype(F32))
    by_owner = (iota((gores, listed), 0).astype(F32) == owner_f).astype(F32)
    before = (iota((listed, listed), 0) < iota((listed, listed), 1)).astype(F32)
    rank = exact_dot(by_owner, before)
    by_row = (iota((listed, rows), 1).astype(F32) == picked_col).astype(F32)
    taken_slots = [jnp.where(rank == float(slot), by_owner, 0.0) for slot in range(2)]
    select = exact_dot(jnp.concatenate(taken_slots, axis=0), by_row).astype(BF16)
    for slot in range(2):
        csend[pl.ds(6 + slot, gores, stride=8), :] = jnp.broadcast_to(
            jnp.sum(taken_slots[slot], axis=1, keepdims=True), (gores, LANES)
        )

    wait_all(inbox, 7, 1)

    def z_copies(step, c):
        up_copy = pltpu.make_async_remote_copy(
            v.at[step, c, cz], v.at[step, c, 0], zs_sem.at[step, 0, c], zr_sem.at[step, 0, c],
            device_id=(lax.rem(s + 1, slabs), g), device_id_type=MESH,
        )
        down_copy = pltpu.make_async_remote_copy(
            v.at[step, c, 1], v.at[step, c, cz + 1], zs_sem.at[step, 1, c], zr_sem.at[step, 1, c],
            device_id=(lax.rem(s + slabs - 1, slabs), g), device_id_type=MESH,
        )
        return up_copy, down_copy

    def y_copies(step, c):
        up_copy = pltpu.make_async_remote_copy(
            ys.at[step, 0, c], yh.at[step, 0, c], ysend_sem.at[step, 0, c], yr_sem.at[step, 0, c],
            device_id=(s, lax.rem(g + 1, gores)), device_id_type=MESH,
        )
        down_copy = pltpu.make_async_remote_copy(
            ys.at[step, 1, c], yh.at[step, 1, c], ysend_sem.at[step, 1, c], yr_sem.at[step, 1, c],
            device_id=(s, lax.rem(g + gores - 1, gores)), device_id_type=MESH,
        )
        return up_copy, down_copy

    def start_pair(pair, at, length):
        @pl.when(at < length - 1)
        def _():
            pair[0].start()

        @pl.when(at > 0)
        def _():
            pair[1].start()

    def recv_pair(pair, at, length):
        @pl.when(at > 0)
        def _():
            pair[0].wait_recv()

        @pl.when(at < length - 1)
        def _():
            pair[1].wait_recv()

    def sent_pair(pair, at, length):
        @pl.when(at < length - 1)
        def _():
            pair[0].wait_send()

        @pl.when(at > 0)
        def _():
            pair[1].wait_send()

    meta = inbox[pl.ds(6, devices, stride=8), :]
    meta_t = meta.T
    line_t = jnp.concatenate(
        [meta_t[0:1, :], meta_t[LANES // 2:LANES // 2 + 1, :]], axis=1
    )
    parts = []
    for c in range(3):
        tiles = jnp.concatenate(
            [inbox[pl.ds(3 * slot + c, devices, stride=8), :] for slot in range(2)], axis=0
        )
        parts.append(jnp.concatenate(split(tiles), axis=1))
    edge_row = iota((2 * cy, 2 * devices), 0)
    edge_row = edge_row + jnp.where(edge_row < cy, 0, (cz - 2) * cy)
    edge_line = (edge_row * nbx + 1).astype(F32)
    edge_hot = jnp.concatenate(
        [
            jnp.where(line_t == edge_line + float(x), 1.0, 0.0).astype(BF16)
            for x in range(nbx)
        ],
        axis=0,
    )
    for c in range(3):
        loads[c].wait()
        added = dot(edge_hot, parts[c])
        added = added[:, :LANES] + added[:, LANES:]
        for x in range(nbx):
            cols = pl.ds(x * LANES, LANES)
            for i, z in enumerate((1, cz)):
                start = (2 * x + i) * cy
                v[0, c, z, :, cols] = v[0, c, z, :, cols] + added[start:start + cy]
        start_pair(z_copies(0, c), s, slabs)
    inner_rows = (cz - 2) * cy
    inner_line = ((iota((inner_rows, 2 * devices), 0) + cy) * nbx + 1).astype(F32)
    for c in range(3):
        for x in range(nbx):
            if c == 0:
                hot_t[x] = jnp.where(line_t == inner_line + float(x), 1.0, 0.0).astype(BF16)
            added = dot(hot_t[x], parts[c])
            added = added[:, :LANES] + added[:, LANES:]
            cols = pl.ds(x * LANES, LANES)
            here = v[0, c, pl.ds(2, cz - 2), :, cols]
            v[0, c, pl.ds(2, cz - 2), :, cols] = here + added.reshape(cz - 2, cy, LANES)
        for z in range(cz):
            ys[0, 0, c, z:z + 1, :] = v[0, c, z + 1, cy - 1:cy, :]
            ys[0, 1, c, z:z + 1, :] = v[0, c, z + 1, 0:1, :]
        start_pair(y_copies(0, c), g, gores)
    loads[3].wait()

    def neighbours(mid, to_right, to_left, left, right, base):
        below, above = lax.rem(s + 1, slabs), lax.rem(s + slabs - 1, slabs)
        after, before = lax.rem(g + 1, gores), lax.rem(g + gores - 1, gores)
        over, under = pl.ds(0, HALO), pl.ds(rows + HALO, HALO)
        head, tail = pl.ds(0, HALO), pl.ds(rows - HALO, HALO)
        plan = (
            (mid.at[:, pl.ds(rows, HALO)], mid.at[:, over], (below, g)),
            (mid.at[:, pl.ds(HALO, HALO)], mid.at[:, under], (above, g)),
            (to_right.at[tail], left.at[over], (below, after)),
            (to_left.at[tail], right.at[over], (below, before)),
            (to_right.at[head], left.at[under], (above, after)),
            (to_left.at[head], right.at[under], (above, before)),
            (to_right, left.at[own], (s, after)),
            (to_left, right.at[own], (s, before)),
        )
        return [
            pltpu.make_async_remote_copy(
                src, to, mem_s.at[base + i], mem_r.at[base + i],
                device_id=where, device_id_type=MESH,
            )
            for i, (src, to, where) in enumerate(plan)
        ]

    band = lax.div(iota((rows, LANES), 1), HALO)

    def pack(mid, to_right, to_left, count):
        going_right = jnp.zeros((rows, LANES), F32)
        going_left = jnp.zeros((rows, LANES), F32)
        for i in range(count):
            part = mid[i, own, :]
            going_right = jnp.where(
                band == i, pltpu.roll(part, HALO * (i + 1), 1), going_right
            )
            moved = part if i == 0 else pltpu.roll(part, HALO * i, 1)
            going_left = jnp.where(band == i, moved, going_left)
        to_right[...] = going_right
        to_left[...] = going_left

    wide = iota((rows + 2 * HALO, LANES), 1)

    def unpack(mid, left, right, i):
        from_left = pltpu.roll(left[...], LANES - HALO * (i + 1), 1)
        from_right = right[...] if i == 0 else pltpu.roll(right[...], LANES - HALO * i, 1)
        side = jnp.where(wide < HALO, from_right, 0.0)
        side = jnp.where(wide >= LANES - HALO, from_left, side)
        return mid[i], side

    pack(sc, spr, spl, 7)
    static_halos = neighbours(sc, spr, spl, sl, sr, 0)

    at_line = (iota((devices, zy), 1) * nbx + 1).astype(F32)
    for slot in range(2):
        named = jnp.broadcast_to(
            meta[:, slot * (LANES // 2):slot * (LANES // 2) + 1], (devices, zy)
        )
        for x in range(nbx):
            hot[x, slot * devices:(slot + 1) * devices, :] = jnp.where(
                named == at_line + float(x), 1.0, 0.0
            ).astype(BF16)

    sub = iota((8, nx), 0)
    lan = iota((8, nx), 1)

    def plane(step, c, z, stage):
        blocks = cy // 8
        center = v[step, c, z + 1, pl.ds(0, 8), :]
        up_roll = jnp.broadcast_to(yh[step, 0, c, pl.ds(z, 1), :], (8, nx))
        down_roll = pltpu.roll(center, 7, 0)
        for yb in range(blocks):
            at = pl.ds(8 * yb, 8)
            rolled = pltpu.roll(center, 1, 0)
            upper = jnp.where(sub == 0, up_roll, rolled)
            if yb + 1 < blocks:
                following = v[step, c, z + 1, pl.ds(8 * yb + 8, 8), :]
                next_roll = pltpu.roll(following, 7, 0)
            else:
                following = None
                next_roll = jnp.broadcast_to(yh[step, 1, c, pl.ds(z, 1), :], (8, nx))
            lower = jnp.where(sub == 7, next_roll, down_roll)
            total = v[step, c, z, at, :] + v[step, c, z + 2, at, :]
            total = total + upper + lower
            total = total + jnp.where(lan == 0, 0.0, pltpu.roll(center, 1, 1))
            total = total + jnp.where(lan == nx - 1, 0.0, pltpu.roll(center, nx - 1, 1))
            new = center + vis[z, at, :] * (total - 6.0 * center)
            if stage:
                v[step + 1, c, z + 1, at, :] = new
            else:
                fluid_out[c, z, at, :] = new
            if stage and yb == 0:
                ys[step + 1, 1, c, pl.ds(z, 1), :] = new[0:1, :]
            if stage and yb == blocks - 1:
                ys[step + 1, 0, c, pl.ds(z, 1), :] = new[7:8, :]
            center, up_roll, down_roll = following, rolled, next_roll

    def substep(step, c, stage):
        recv_pair(y_copies(step, c), g, gores)

        def inner(z, carry):
            plane(step, c, z, stage)
            return carry

        lax.fori_loop(1, cz - 1, inner, 0)
        recv_pair(z_copies(step, c), s, slabs)
        plane(step, c, 0, stage)
        plane(step, c, cz - 1, stage)
        if stage:
            start_pair(z_copies(step + 1, c), s, slabs)
            start_pair(y_copies(step + 1, c), g, gores)

    def early(i, carry):
        substep(lax.div(i, 3), lax.rem(i, 3), True)
        return carry

    lax.fori_loop(0, 3 * (STEPS - 1), early, 0)
    for copy in static_halos:
        copy.start()

    def last(c, carry):
        substep(STEPS - 1, c, False)
        sampled = jnp.zeros((2 * devices, 2 * LANES), F32)
        for x in range(nbx):
            cell = fluid_out[c, :, :, pl.ds(x * LANES, LANES)].reshape(zy, LANES)
            sampled = sampled + dot(hot[x], jnp.concatenate(split(cell), axis=1))
        sampled = sampled[:, :LANES] + sampled[:, LANES:]
        for slot in range(2):
            ansbox[pl.ds(3 * slot + c, devices, stride=8), :] = (
                sampled[slot * devices:(slot + 1) * devices]
            )
        return carry

    lax.fori_loop(0, 3, last, 0)

    retbox[rows_of(me, 8), :] = ansbox[rows_of(me, 8), :]
    send_all(ansbox, retbox, 6, 2)
    wait_all(retbox, 6, 3)
    for c in range(3):
        hi, lo = split(
            jnp.concatenate(
                [retbox[pl.ds(3 * slot + c, devices, stride=8), :] for slot in range(2)], axis=0
            )
        )
        taken = dot(back_pick, hi) + dot(back_pick, lo)
        node_velocity = (taken[:rows] + taken[rows:]) * 0.5
        dc[c, own, :] = (canopy[c] + node_velocity) * inv[...]

    moving_halos = neighbours(dc, dpr, dpl, dl, dr, 8)
    for copy in moving_halos[:2]:
        copy.start()
    pack(dc, dpr, dpl, 3)
    for copy in moving_halos[2:]:
        copy.start()

    for copy in static_halos:
        copy.wait_recv()
    for i in range(7):
        middle, side = unpack(sc, sl, sr, i)
        ext[i, :, 0:LANES] = middle
        ext[i, :, LANES:2 * LANES] = side
    for copy in moving_halos:
        copy.wait_recv()
    for c in range(3):
        middle, side = unpack(dc, dl, dr, c)
        ext[7 + c, :, 0:LANES] = middle
        ext[7 + c, :, LANES:2 * LANES] = side

    height = rows + 2 * HALO

    def sweep(i, carry):
        for c in range(3):
            p = ext[4 + c]
            new = ext[7 + c] + ext[0] * pltpu.roll(p, 1, 0)
            new = new + ext[1] * pltpu.roll(p, height - 1, 0)
            new = new + ext[2] * pltpu.roll(p, 1, 1)
            new = new + ext[3] * pltpu.roll(p, 2 * LANES - 1, 1)
            ext[4 + c] = new
        return carry

    lax.fori_loop(0, SWEEPS, sweep, 0)

    for c in range(3):
        patch = ext[4 + c, own, 0:LANES]
        canopy_out[c] = patch
        hi, mid = split(patch)
        low = (patch - hi.astype(F32) - mid.astype(F32)).astype(BF16)
        chosen = dot(select, jnp.concatenate([hi, mid, low], axis=1))
        chosen = chosen[:, :LANES] + chosen[:, LANES:2 * LANES] + chosen[:, 2 * LANES:]
        for slot in range(2):
            csend[pl.ds(3 * slot + c, gores, stride=8), :] = (
                chosen[slot * gores:(slot + 1) * gores]
            )
    mine = pl.ds(pl.multiple_of(g * 8, 8), 8)
    crecv[mine, :] = csend[mine, :]
    for i in range(1, gores):
        t = lax.rem(g + i, gores)
        pltpu.make_async_remote_copy(
            csend.at[pl.ds(pl.multiple_of(t * 8, 8), 8)], crecv.at[mine],
            con_sem.at[0], con_sem.at[1], device_id=(s, t), device_id_type=MESH,
        ).start()
    most = pl.ds(0, (gores - 1) * 8)
    pltpu.make_async_copy(crecv.at[most], crecv.at[most], con_sem.at[1]).wait()
    sets_out[...] = crecv[...]

    pltpu.make_async_copy(csend.at[most], csend.at[most], con_sem.at[0]).wait()
    wait_all(outbox, 7, 0)
    wait_all(ansbox, 6, 2)
    for copy in static_halos + moving_halos:
        copy.wait_send()

    def drain(i, carry):
        step, c = lax.div(i, 3), lax.rem(i, 3)
        sent_pair(z_copies(step, c), s, slabs)
        sent_pair(y_copies(step, c), g, gores)
        return carry

    lax.fori_loop(0, 3 * STEPS, drain, 0)


def contact_kernel(
    gores, fluid_in, canopy_in, sets, fluid_out, canopy_out, force, xj, fj, acc_ref, pad, sem
):
    stores = (
        pltpu.make_async_copy(fluid_in, fluid_out, sem.at[0]),
        pltpu.make_async_copy(canopy_in, canopy_out, sem.at[1]),
    )
    for store in stores:
        store.start()
    slots = 2 * gores
    group = 8
    pad[...] = jnp.zeros_like(pad)
    for a in range(slots):
        base = (a // 2) * 8
        flag = sets[base + 6 + a % 2:base + 7 + a % 2, :]
        for c in range(3):
            k = c * slots + a
            row = base + 3 * (a % 2) + c
            point = jnp.where(flag > 0.0, sets[row:row + 1, :], FAR)
            pad[k:k + 1, :] = point
            xj[k] = jnp.broadcast_to(point, (8, LANES))
    points_t = pad[...].T
    pad[...] = points_t
    fj[...] = jnp.zeros_like(fj)

    def block(i, carry):
        at = [pl.ds(pl.multiple_of((i * group + t) * 8, 8), 8) for t in range(group)]
        column = [pad[rows, :] for rows in at]
        for a in range(slots - 2):
            xi = [
                [
                    jnp.broadcast_to(
                        column[t][:, c * slots + a:c * slots + a + 1], (8, LANES)
                    )
                    for c in range(3)
                ]
                for t in range(group)
            ]
            acc = [[None] * 3 for _ in range(group)]
            for b in range(2 * (a // 2) + 2, slots):
                other = [xj[c * slots + b] for c in range(3)]
                pushed = [None] * 3
                for t in range(group):
                    d = [xi[t][c] - other[c] for c in range(3)]
                    square = d[0] * d[0] + d[1] * d[1] + (d[2] * d[2] + SOFTEN)
                    inverse = lax.rsqrt(square)
                    gap = jnp.maximum(REACH - square * inverse, 0.0)
                    weight = gap * gap * inverse
                    for c in range(3):
                        push = weight * d[c]
                        acc[t][c] = push if acc[t][c] is None else acc[t][c] + push
                        pushed[c] = push if pushed[c] is None else pushed[c] + push
                for c in range(3):
                    fj[c * slots + b] = fj[c * slots + b] + pushed[c]
            for t in range(group):
                for c in range(3):
                    acc_ref[c * slots + a, at[t], :] = acc[t][c]
        return carry

    lax.fori_loop(0, LANES // (8 * group), block, 0)
    for c in range(3):
        for a in range(slots):
            k = c * slots + a
            total = -jnp.sum(fj[k], axis=0, keepdims=True)
            if a < slots - 2:
                total = total + jnp.sum(acc_ref[k].T, axis=0, keepdims=True)
            force[c, a:a + 1, :] = GAIN * total
    for store in stores:
        store.wait()


def body(
    slabs, gores,
    fluid_velocity, viscosity, pressure_jump, normals, canopy_position, tension,
    slot_cut, couple_dest, couple_block, contact_owner, contact_row,
):
    cz, cy, nx = viscosity.shape
    rows = pressure_jump.shape[0]
    devices = slabs * gores
    zy = cz * cy
    nbx = nx // LANES
    vmem = pl.BlockSpec(memory_space=pltpu.VMEM)
    anywhere = pl.BlockSpec(memory_space=pl.ANY)
    dma = pltpu.SemaphoreType.DMA
    cut_width = min(LANES, slot_cut.shape[0])
    tall = rows + 2 * HALO
    fluid, canopy, sets = pl.pallas_call(
        functools.partial(main_kernel, slabs, gores),
        out_shape=(
            jax.ShapeDtypeStruct(fluid_velocity.shape, F32),
            jax.ShapeDtypeStruct(canopy_position.shape, F32),
            jax.ShapeDtypeStruct((gores * 8, LANES), F32),
        ),
        in_specs=[pl.BlockSpec(memory_space=pltpu.HBM)] * 11,
        out_specs=(vmem, vmem, vmem),
        scratch_shapes=[
            pltpu.VMEM(pressure_jump.shape, F32),
            pltpu.VMEM(normals.shape, F32),
            pltpu.VMEM(canopy_position.shape, F32),
            pltpu.VMEM(tension.shape, F32),
            pltpu.VMEM((slot_cut.shape[0] // cut_width, cut_width), jnp.int32),
            pltpu.VMEM((2, rows), jnp.int32),
            pltpu.VMEM((2, rows), jnp.int32),
            pltpu.VMEM(contact_row.shape, jnp.int32),
            pltpu.VMEM(contact_row.shape, jnp.int32),
            pltpu.VMEM((STEPS, 3, cz + 2, cy, nx), F32),
            pltpu.VMEM((cz, cy, nx), F32),
            pltpu.VMEM((STEPS, 2, 3, cz, nx), F32),
            pltpu.VMEM((STEPS, 2, 3, cz, nx), F32),
            pltpu.VMEM((devices * 8, LANES), F32),
            pltpu.VMEM((devices * 8, LANES), F32),
            pltpu.VMEM((devices * 8, LANES), F32),
            pltpu.VMEM((devices * 8, LANES), F32),
            pltpu.VMEM((nbx, zy - 2 * (zy // cz), 2 * devices), BF16),
            pltpu.VMEM((nbx, 2 * devices, zy), BF16),
            pltpu.VMEM((7, tall, LANES), F32),
            pltpu.VMEM((rows, LANES), F32),
            pltpu.VMEM((rows, LANES), F32),
            pltpu.VMEM((tall, LANES), F32),
            pltpu.VMEM((tall, LANES), F32),
            pltpu.VMEM((3, tall, LANES), F32),
            pltpu.VMEM((rows, LANES), F32),
            pltpu.VMEM((rows, LANES), F32),
            pltpu.VMEM((tall, LANES), F32),
            pltpu.VMEM((tall, LANES), F32),
            pltpu.VMEM((10, tall, 2 * LANES), F32),
            pltpu.VMEM((rows, LANES), F32),
            pltpu.VMEM((gores * 8, LANES), F32),
            pltpu.VMEM((gores * 8, LANES), F32),
            dma((9,)),
            dma((4,)),
            dma((STEPS, 2, 3)),
            dma((STEPS, 2, 3)),
            dma((STEPS, 2, 3)),
            dma((STEPS, 2, 3)),
            dma((4,)),
            dma((16,)),
            dma((16,)),
            dma((2,)),
        ],
        compiler_params=pltpu.CompilerParams(
            collective_id=0, has_side_effects=True, vmem_limit_bytes=26 << 20
        ),
        name="fluid_membrane",
    )(*(
        pltpu.with_memory_space_constraint(x, pltpu.HBM)
        for x in (
            fluid_velocity, viscosity, pressure_jump, normals, canopy_position, tension,
            slot_cut.reshape(-1, cut_width),
            couple_dest[0].T, couple_block[0].T, contact_owner[:, :, 0], contact_row,
        )
    ))
    slots = 2 * gores
    fluid, canopy, force = pl.pallas_call(
        functools.partial(contact_kernel, gores),
        out_shape=(
            jax.ShapeDtypeStruct(fluid.shape, F32),
            jax.ShapeDtypeStruct(canopy.shape, F32),
            jax.ShapeDtypeStruct((3, slots, LANES), F32),
        ),
        in_specs=[vmem, vmem, vmem],
        out_specs=(anywhere, anywhere, vmem),
        scratch_shapes=[
            pltpu.VMEM((3 * slots, 8, LANES), F32),
            pltpu.VMEM((3 * slots, 8, LANES), F32),
            pltpu.VMEM((3 * slots, LANES, LANES), F32),
            pltpu.VMEM((LANES, LANES), F32),
            dma((2,)),
        ],
        compiler_params=pltpu.CompilerParams(vmem_limit_bytes=12 << 20),
        name="contact",
    )(fluid, canopy, sets)
    return fluid, canopy, jnp.swapaxes(force, 0, 1)[None, None]


def solution(mesh):
    in_specs = (
        P(None, "slab", "gore", None),
        P("slab", "gore", None),
        P("slab", "gore"),
        P(None, "slab", "gore"),
        P(None, "slab", "gore"),
        P(None, "slab", "gore"),
        P(),
        P("gore", "slab", None),
        P("gore", "slab", None),
        P("gore", "slab", None),
        P("gore", "slab"),
    )
    out_specs = (
        P(None, "slab", "gore", None),
        P(None, "slab", "gore"),
        P("slab", "gore", None, None, None),
    )
    step = functools.partial(body, mesh.shape["slab"], mesh.shape["gore"])
    return jax.shard_map(step, mesh=mesh, in_specs=in_specs, out_specs=out_specs, check_vma=False)
```

```python
import functools

import jax
import jax.numpy as jnp
from jax import lax
from jax.experimental import pallas as pl
from jax.experimental.pallas import tpu as pltpu
from jax.sharding import PartitionSpec as P

STEPS = 3
SWEEPS = 8
HALO = 8
LANES = 128
GAIN = 0.1
REACH = 1.0
SOFTEN = 0.01
FAR = 1.0e15
MESH = pl.DeviceIdType.MESH
F32 = jnp.float32
BF16 = jnp.bfloat16


def iota(shape, dim):
    return lax.broadcasted_iota(jnp.int32, shape, dim)


def dot(a, b):
    return lax.dot_general(a, b, (((1,), (0,)), ((), ())), preferred_element_type=F32)


def exact_dot(a, b):
    return lax.dot_general(
        a, b, (((1,), (0,)), ((), ())),
        precision=lax.Precision.HIGHEST, preferred_element_type=F32,
    )


def split(x):
    hi = x.astype(BF16)
    return hi, (x - hi.astype(F32)).astype(BF16)


def to_column(row):
    n = row.shape[1]
    same = iota((n, n), 0) == iota((n, n), 1)
    return jnp.sum(jnp.where(same, jnp.broadcast_to(row, (n, n)), 0.0), axis=1, keepdims=True)


def main_kernel(
    slabs, gores,
    fluid_hbm, visc_hbm, jump_hbm, normals_hbm, canopy_hbm, tension_hbm, cut_hbm,
    dest_hbm, block_hbm, owner_hbm, picked_hbm,
    fluid_out, canopy_out, sets_out,
    jump, normals, canopy, tension, cut, dest, block, owner, picked,
    v, vis, yh, ys, outbox, inbox, ansbox, retbox, hot_t, hot,
    sc, spr, spl, sl, sr, dc, dpr, dpl, dl, dr, ext, inv, csend, crecv,
    small_sem, load_sem, zs_sem, zr_sem, ysend_sem, yr_sem, a2a_sem, mem_s, mem_r, con_sem,
):
    s = lax.axis_index("slab")
    g = lax.axis_index("gore")
    me = s * gores + g
    devices = slabs * gores
    cz, cy, nx = vis.shape
    zy = cz * cy
    nbx = nx // LANES
    rows = jump.shape[0]

    def device(t):
        return (lax.div(t, gores), lax.rem(t, gores))

    def rows_of(t, count):
        return pl.ds(pl.multiple_of(t * 8, 8), count)

    loads = [
        pltpu.make_async_copy(fluid_hbm.at[c], v.at[0, c, pl.ds(1, cz)], load_sem.at[c])
        for c in range(3)
    ]
    loads.append(pltpu.make_async_copy(visc_hbm, vis, load_sem.at[3]))
    small = [
        pltpu.make_async_copy(src, dst, small_sem.at[i])
        for i, (src, dst) in enumerate((
            (dest_hbm, dest), (block_hbm, block), (jump_hbm, jump), (normals_hbm, normals),
            (canopy_hbm, canopy), (tension_hbm, tension), (cut_hbm, cut),
            (owner_hbm, owner), (picked_hbm, picked),
        ))
    ]
    for copy in small + loads:
        copy.start()
    barrier = pltpu.get_barrier_semaphore()

    def greet(i, carry):
        t = lax.rem(me + i, devices)
        pl.semaphore_signal(barrier, inc=1, device_id=device(t), device_id_type=MESH)
        return carry

    lax.fori_loop(1, devices, greet, 0)

    for copy in small:
        copy.wait()

    dest_row = jnp.concatenate([dest[0:1, :], dest[1:2, :]], axis=1).astype(F32)
    line_row = jnp.concatenate([block[0:1, :], block[1:2, :]], axis=1).astype(F32)
    entries = 2 * rows
    dest_col = to_column(dest_row)
    line_col = to_column(line_row) + 1.0
    by_dev = (iota((devices, entries), 0).astype(F32) == dest_row).astype(F32)
    by_entry = (iota((entries, devices), 1).astype(F32) == dest_col).astype(F32)
    row_a = lax.rem(iota((entries, entries), 0), rows)
    row_b = lax.rem(iota((entries, entries), 1), rows)
    rank_dev = dot(by_dev.astype(BF16), (row_a < row_b).astype(BF16))
    rank_entry = dot((row_b < row_a).astype(BF16), by_entry.astype(BF16))
    surface = [jump[...] * normals[c] * 0.25 for c in range(3)]
    columns = [jnp.concatenate([t, t], axis=0) for t in surface]
    columns.append(jnp.broadcast_to(line_col, (entries, LANES)))
    table = jnp.concatenate(columns, axis=1)
    table_hi, table_lo = split(table)
    pick = jnp.concatenate(
        [jnp.where(rank_dev == float(slot), by_dev, 0.0) for slot in range(2)], axis=0
    ).astype(BF16)
    placed = dot(pick, table_hi) + dot(pick, table_lo)
    for slot in range(2):
        for c in range(3):
            outbox[pl.ds(3 * slot + c, devices, stride=8), :] = (
                placed[slot * devices:(slot + 1) * devices, c * LANES:(c + 1) * LANES]
            )
    outbox[pl.ds(6, devices, stride=8), :] = jnp.where(
        iota((devices, LANES), 1) < LANES // 2,
        placed[:devices, 3 * LANES:], placed[devices:, 3 * LANES:],
    )
    back_pick = jnp.concatenate(
        [jnp.where(rank_entry == float(slot), by_entry, 0.0) for slot in range(2)], axis=1
    ).astype(BF16)

    pl.semaphore_wait(barrier, devices - 1)
    inbox[rows_of(me, 8), :] = outbox[rows_of(me, 8), :]

    def send_all(source, target, count, sem):
        def one(i, carry):
            t = lax.rem(me + i, devices)
            pltpu.make_async_remote_copy(
                source.at[rows_of(t, count)], target.at[rows_of(me, count)],
                a2a_sem.at[sem], a2a_sem.at[sem + 1],
                device_id=device(t), device_id_type=MESH,
            ).start()
            return carry

        lax.fori_loop(1, devices, one, 0)

    def wait_all(buffer, count, sem):
        part = buffer.at[pl.ds(0, (devices - 1) * count)]
        pltpu.make_async_copy(part, part, a2a_sem.at[sem]).wait()

    send_all(outbox, inbox, 7, 0)

    zero_plane = jnp.zeros((cy, nx), F32)
    zero_edge = jnp.zeros((cz, nx), F32)

    @pl.when(s == 0)
    def _():
        for step in range(STEPS):
            for c in range(3):
                v[step, c, 0] = zero_plane

    @pl.when(s == slabs - 1)
    def _():
        for step in range(STEPS):
            for c in range(3):
                v[step, c, cz + 1] = zero_plane

    @pl.when(g == 0)
    def _():
        for step in range(STEPS):
            for c in range(3):
                yh[step, 0, c] = zero_edge

    @pl.when(g == gores - 1)
    def _():
        for step in range(STEPS):
            for c in range(3):
                yh[step, 1, c] = zero_edge

    first = s * rows
    cut_f = cut[...].astype(F32)
    cut_rows, cut_width = cut.shape
    node = first + iota((rows, cut_width), 0)
    lane = iota((rows, cut_width), 1)
    down = jnp.zeros((rows, cut_width), F32)
    up = jnp.zeros((rows, cut_width), F32)
    total_rows = slabs * rows
    for q in range(cut_rows):
        index = q * cut_width + lane
        keep = jnp.broadcast_to(1.0 - cut_f[q:q + 1, :], (rows, cut_width))
        down += jnp.where((index == node) & (index < total_rows - 1), keep, 0.0)
        up += jnp.where(index == node - 1, keep, 0.0)
    keep_down = jnp.sum(down, axis=1, keepdims=True)
    keep_up = jnp.sum(up, axis=1, keepdims=True)
    w_up = tension[0] * keep_up
    w_down = tension[1] * keep_down
    w_left = tension[2]
    w_right = tension[3]
    scale = 1.0 / (1.0 + w_up + w_down + w_left + w_right)
    inv[...] = scale
    own = pl.ds(HALO, rows)
    for i, w in enumerate((w_up, w_down, w_left, w_right)):
        sc[i, own, :] = w * scale
    for c in range(3):
        sc[4 + c, own, :] = canopy[c]

    listed = owner.shape[1]
    owner_f = owner[...].astype(F32)
    picked_col = to_column(picked[...].astype(F32))
    by_owner = (iota((gores, listed), 0).astype(F32) == owner_f).astype(F32)
    before = (iota((listed, listed), 0) < iota((listed, listed), 1)).astype(F32)
    rank = exact_dot(by_owner, before)
    by_row = (iota((listed, rows), 1).astype(F32) == picked_col).astype(F32)
    taken_slots = [jnp.where(rank == float(slot), by_owner, 0.0) for slot in range(2)]
    select = exact_dot(jnp.concatenate(taken_slots, axis=0), by_row).astype(BF16)
    for slot in range(2):
        csend[pl.ds(6 + slot, gores, stride=8), :] = jnp.broadcast_to(
            jnp.sum(taken_slots[slot], axis=1, keepdims=True), (gores, LANES)
        )

    wait_all(inbox, 7, 1)

    def z_copies(step, c):
        up_copy = pltpu.make_async_remote_copy(
            v.at[step, c, cz], v.at[step, c, 0], zs_sem.at[step, 0, c], zr_sem.at[step, 0, c],
            device_id=(lax.rem(s + 1, slabs), g), device_id_type=MESH,
        )
        down_copy = pltpu.make_async_remote_copy(
            v.at[step, c, 1], v.at[step, c, cz + 1], zs_sem.at[step, 1, c], zr_sem.at[step, 1, c],
            device_id=(lax.rem(s + slabs - 1, slabs), g), device_id_type=MESH,
        )
        return up_copy, down_copy

    def y_copies(step, c):
        up_copy = pltpu.make_async_remote_copy(
            ys.at[step, 0, c], yh.at[step, 0, c], ysend_sem.at[step, 0, c], yr_sem.at[step, 0, c],
            device_id=(s, lax.rem(g + 1, gores)), device_id_type=MESH,
        )
        down_copy = pltpu.make_async_remote_copy(
            ys.at[step, 1, c], yh.at[step, 1, c], ysend_sem.at[step, 1, c], yr_sem.at[step, 1, c],
            device_id=(s, lax.rem(g + gores - 1, gores)), device_id_type=MESH,
        )
        return up_copy, down_copy

    def start_pair(pair, at, length):
        @pl.when(at < length - 1)
        def _():
            pair[0].start()

        @pl.when(at > 0)
        def _():
            pair[1].start()

    def recv_pair(pair, at, length):
        @pl.when(at > 0)
        def _():
            pair[0].wait_recv()

        @pl.when(at < length - 1)
        def _():
            pair[1].wait_recv()

    def sent_pair(pair, at, length):
        @pl.when(at < length - 1)
        def _():
            pair[0].wait_send()

        @pl.when(at > 0)
        def _():
            pair[1].wait_send()

    meta = inbox[pl.ds(6, devices, stride=8), :]
    meta_t = meta.T
    line_t = jnp.concatenate(
        [meta_t[0:1, :], meta_t[LANES // 2:LANES // 2 + 1, :]], axis=1
    )
    parts = []
    for c in range(3):
        tiles = jnp.concatenate(
            [inbox[pl.ds(3 * slot + c, devices, stride=8), :] for slot in range(2)], axis=0
        )
        parts.append(jnp.concatenate(split(tiles), axis=1))
    edge_row = iota((2 * cy, 2 * devices), 0)
    edge_row = edge_row + jnp.where(edge_row < cy, 0, (cz - 2) * cy)
    edge_line = (edge_row * nbx + 1).astype(F32)
    edge_hot = jnp.concatenate(
        [
            jnp.where(line_t == edge_line + float(x), 1.0, 0.0).astype(BF16)
            for x in range(nbx)
        ],
        axis=0,
    )
    for c in range(3):
        loads[c].wait()
        added = dot(edge_hot, parts[c])
        added = added[:, :LANES] + added[:, LANES:]
        for x in range(nbx):
            cols = pl.ds(x * LANES, LANES)
            for i, z in enumerate((1, cz)):
                start = (2 * x + i) * cy
                v[0, c, z, :, cols] = v[0, c, z, :, cols] + added[start:start + cy]
        start_pair(z_copies(0, c), s, slabs)
    inner_rows = (cz - 2) * cy
    inner_line = ((iota((inner_rows, 2 * devices), 0) + cy) * nbx + 1).astype(F32)
    for c in range(3):
        for x in range(nbx):
            if c == 0:
                hot_t[x] = jnp.where(line_t == inner_line + float(x), 1.0, 0.0).astype(BF16)
            added = dot(hot_t[x], parts[c])
            added = added[:, :LANES] + added[:, LANES:]
            cols = pl.ds(x * LANES, LANES)
            here = v[0, c, pl.ds(2, cz - 2), :, cols]
            v[0, c, pl.ds(2, cz - 2), :, cols] = here + added.reshape(cz - 2, cy, LANES)
        for z in range(cz):
            ys[0, 0, c, z:z + 1, :] = v[0, c, z + 1, cy - 1:cy, :]
            ys[0, 1, c, z:z + 1, :] = v[0, c, z + 1, 0:1, :]
        start_pair(y_copies(0, c), g, gores)
    loads[3].wait()

    def neighbours(mid, to_right, to_left, left, right, base):
        below, above = lax.rem(s + 1, slabs), lax.rem(s + slabs - 1, slabs)
        after, before = lax.rem(g + 1, gores), lax.rem(g + gores - 1, gores)
        over, under = pl.ds(0, HALO), pl.ds(rows + HALO, HALO)
        head, tail = pl.ds(0, HALO), pl.ds(rows - HALO, HALO)
        plan = (
            (mid.at[:, pl.ds(rows, HALO)], mid.at[:, over], (below, g)),
            (mid.at[:, pl.ds(HALO, HALO)], mid.at[:, under], (above, g)),
            (to_right.at[tail], left.at[over], (below, after)),
            (to_left.at[tail], right.at[over], (below, before)),
            (to_right.at[head], left.at[under], (above, after)),
            (to_left.at[head], right.at[under], (above, before)),
            (to_right, left.at[own], (s, after)),
            (to_left, right.at[own], (s, before)),
        )
        return [
            pltpu.make_async_remote_copy(
                src, to, mem_s.at[base + i], mem_r.at[base + i],
                device_id=where, device_id_type=MESH,
            )
            for i, (src, to, where) in enumerate(plan)
        ]

    band = lax.div(iota((rows, LANES), 1), HALO)

    def pack(mid, to_right, to_left, count):
        going_right = jnp.zeros((rows, LANES), F32)
        going_left = jnp.zeros((rows, LANES), F32)
        for i in range(count):
            part = mid[i, own, :]
            going_right = jnp.where(
                band == i, pltpu.roll(part, HALO * (i + 1), 1), going_right
            )
            moved = part if i == 0 else pltpu.roll(part, HALO * i, 1)
            going_left = jnp.where(band == i, moved, going_left)
        to_right[...] = going_right
        to_left[...] = going_left

    wide = iota((rows + 2 * HALO, LANES), 1)

    def unpack(mid, left, right, i):
        from_left = pltpu.roll(left[...], LANES - HALO * (i + 1), 1)
        from_right = right[...] if i == 0 else pltpu.roll(right[...], LANES - HALO * i, 1)
        side = jnp.where(wide < HALO, from_right, 0.0)
        side = jnp.where(wide >= LANES - HALO, from_left, side)
        return mid[i], side

    pack(sc, spr, spl, 7)
    static_halos = neighbours(sc, spr, spl, sl, sr, 0)

    at_line = (iota((devices, zy), 1) * nbx + 1).astype(F32)
    for slot in range(2):
        named = jnp.broadcast_to(
            meta[:, slot * (LANES // 2):slot * (LANES // 2) + 1], (devices, zy)
        )
        for x in range(nbx):
            hot[x, slot * devices:(slot + 1) * devices, :] = jnp.where(
                named == at_line + float(x), 1.0, 0.0
            ).astype(BF16)

    sub = iota((8, nx), 0)
    lan = iota((8, nx), 1)

    def plane(step, c, z, stage):
        blocks = cy // 8
        center = v[step, c, z + 1, pl.ds(0, 8), :]
        up_roll = jnp.broadcast_to(yh[step, 0, c, pl.ds(z, 1), :], (8, nx))
        down_roll = pltpu.roll(center, 7, 0)
        for yb in range(blocks):
            at = pl.ds(8 * yb, 8)
            rolled = pltpu.roll(center, 1, 0)
            upper = jnp.where(sub == 0, up_roll, rolled)
            if yb + 1 < blocks:
                following = v[step, c, z + 1, pl.ds(8 * yb + 8, 8), :]
                next_roll = pltpu.roll(following, 7, 0)
            else:
                following = None
                next_roll = jnp.broadcast_to(yh[step, 1, c, pl.ds(z, 1), :], (8, nx))
            lower = jnp.where(sub == 7, next_roll, down_roll)
            total = v[step, c, z, at, :] + v[step, c, z + 2, at, :]
            total = total + upper + lower
            total = total + jnp.where(lan == 0, 0.0, pltpu.roll(center, 1, 1))
            total = total + jnp.where(lan == nx - 1, 0.0, pltpu.roll(center, nx - 1, 1))
            new = center + vis[z, at, :] * (total - 6.0 * center)
            if stage:
                v[step + 1, c, z + 1, at, :] = new
            else:
                fluid_out[c, z, at, :] = new
            if stage and yb == 0:
                ys[step + 1, 1, c, pl.ds(z, 1), :] = new[0:1, :]
            if stage and yb == blocks - 1:
                ys[step + 1, 0, c, pl.ds(z, 1), :] = new[7:8, :]
            center, up_roll, down_roll = following, rolled, next_roll

    def substep(step, c, stage):
        recv_pair(y_copies(step, c), g, gores)

        def inner(z, carry):
            plane(step, c, z, stage)
            return carry

        lax.fori_loop(1, cz - 1, inner, 0)
        recv_pair(z_copies(step, c), s, slabs)
        plane(step, c, 0, stage)
        plane(step, c, cz - 1, stage)
        if stage:
            start_pair(z_copies(step + 1, c), s, slabs)
            start_pair(y_copies(step + 1, c), g, gores)

    def early(i, carry):
        substep(lax.div(i, 3), lax.rem(i, 3), True)
        return carry

    lax.fori_loop(0, 3 * (STEPS - 1), early, 0)
    for copy in static_halos:
        copy.start()

    def last(c, carry):
        substep(STEPS - 1, c, False)
        sampled = jnp.zeros((2 * devices, 2 * LANES), F32)
        for x in range(nbx):
            cell = fluid_out[c, :, :, pl.ds(x * LANES, LANES)].reshape(zy, LANES)
            sampled = sampled + dot(hot[x], jnp.concatenate(split(cell), axis=1))
        sampled = sampled[:, :LANES] + sampled[:, LANES:]
        for slot in range(2):
            ansbox[pl.ds(3 * slot + c, devices, stride=8), :] = (
                sampled[slot * devices:(slot + 1) * devices]
            )
        return carry

    lax.fori_loop(0, 3, last, 0)

    retbox[rows_of(me, 8), :] = ansbox[rows_of(me, 8), :]
    send_all(ansbox, retbox, 6, 2)
    wait_all(retbox, 6, 3)
    for c in range(3):
        hi, lo = split(
            jnp.concatenate(
                [retbox[pl.ds(3 * slot + c, devices, stride=8), :] for slot in range(2)], axis=0
            )
        )
        taken = dot(back_pick, hi) + dot(back_pick, lo)
        node_velocity = (taken[:rows] + taken[rows:]) * 0.5
        dc[c, own, :] = (canopy[c] + node_velocity) * inv[...]

    moving_halos = neighbours(dc, dpr, dpl, dl, dr, 8)
    for copy in moving_halos[:2]:
        copy.start()
    pack(dc, dpr, dpl, 3)
    for copy in moving_halos[2:]:
        copy.start()

    for copy in static_halos:
        copy.wait_recv()
    for i in range(7):
        middle, side = unpack(sc, sl, sr, i)
        ext[i, :, 0:LANES] = middle
        ext[i, :, LANES:2 * LANES] = side
    for copy in moving_halos:
        copy.wait_recv()
    for c in range(3):
        middle, side = unpack(dc, dl, dr, c)
        ext[7 + c, :, 0:LANES] = middle
        ext[7 + c, :, LANES:2 * LANES] = side

    height = rows + 2 * HALO

    def sweep(i, carry):
        for c in range(3):
            p = ext[4 + c]
            new = ext[7 + c] + ext[0] * pltpu.roll(p, 1, 0)
            new = new + ext[1] * pltpu.roll(p, height - 1, 0)
            new = new + ext[2] * pltpu.roll(p, 1, 1)
            new = new + ext[3] * pltpu.roll(p, 2 * LANES - 1, 1)
            ext[4 + c] = new
        return carry

    lax.fori_loop(0, SWEEPS, sweep, 0, unroll=True)

    for c in range(3):
        patch = ext[4 + c, own, 0:LANES]
        canopy_out[c] = patch
        hi, mid = split(patch)
        low = (patch - hi.astype(F32) - mid.astype(F32)).astype(BF16)
        chosen = dot(select, jnp.concatenate([hi, mid, low], axis=1))
        chosen = chosen[:, :LANES] + chosen[:, LANES:2 * LANES] + chosen[:, 2 * LANES:]
        for slot in range(2):
            csend[pl.ds(3 * slot + c, gores, stride=8), :] = (
                chosen[slot * gores:(slot + 1) * gores]
            )
    mine = pl.ds(pl.multiple_of(g * 8, 8), 8)
    crecv[mine, :] = csend[mine, :]
    for i in range(1, gores):
        t = lax.rem(g + i, gores)
        pltpu.make_async_remote_copy(
            csend.at[pl.ds(pl.multiple_of(t * 8, 8), 8)], crecv.at[mine],
            con_sem.at[0], con_sem.at[1], device_id=(s, t), device_id_type=MESH,
        ).start()
    most = pl.ds(0, (gores - 1) * 8)
    pltpu.make_async_copy(crecv.at[most], crecv.at[most], con_sem.at[1]).wait()
    sets_out[...] = crecv[...]

    pltpu.make_async_copy(csend.at[most], csend.at[most], con_sem.at[0]).wait()
    wait_all(outbox, 7, 0)
    wait_all(ansbox, 6, 2)
    for copy in static_halos + moving_halos:
        copy.wait_send()

    def drain(i, carry):
        step, c = lax.div(i, 3), lax.rem(i, 3)
        sent_pair(z_copies(step, c), s, slabs)
        sent_pair(y_copies(step, c), g, gores)
        return carry

    lax.fori_loop(0, 3 * STEPS, drain, 0)


def contact_kernel(
    gores, fluid_in, canopy_in, sets, fluid_out, canopy_out, force, xj, fj, acc_ref, pad, sem
):
    stores = (
        pltpu.make_async_copy(fluid_in, fluid_out, sem.at[0]),
        pltpu.make_async_copy(canopy_in, canopy_out, sem.at[1]),
    )
    for store in stores:
        store.start()
    slots = 2 * gores
    group = 16
    pad[...] = jnp.zeros_like(pad)
    for a in range(slots):
        base = (a // 2) * 8
        flag = sets[base + 6 + a % 2:base + 7 + a % 2, :]
        for c in range(3):
            k = c * slots + a
            row = base + 3 * (a % 2) + c
            point = jnp.where(flag > 0.0, sets[row:row + 1, :], FAR)
            pad[k:k + 1, :] = point
            xj[k] = jnp.broadcast_to(point, (8, LANES))
    points_t = pad[...].T
    pad[...] = points_t
    fj[...] = jnp.zeros_like(fj)

    def block(i, carry):
        at = [pl.ds(pl.multiple_of((i * group + t) * 8, 8), 8) for t in range(group)]
        column = [pad[rows, :] for rows in at]
        for a in range(slots - 2):
            xi = [
                [
                    jnp.broadcast_to(
                        column[t][:, c * slots + a:c * slots + a + 1], (8, LANES)
                    )
                    for c in range(3)
                ]
                for t in range(group)
            ]
            acc = [[None] * 3 for _ in range(group)]
            for b in range(2 * (a // 2) + 2, slots):
                other = [xj[c * slots + b] for c in range(3)]
                pushed = [None] * 3
                for t in range(group):
                    d = [xi[t][c] - other[c] for c in range(3)]
                    square = d[0] * d[0] + d[1] * d[1] + (d[2] * d[2] + SOFTEN)
                    inverse = lax.rsqrt(square)
                    gap = jnp.maximum(REACH - square * inverse, 0.0)
                    weight = gap * gap * inverse
                    for c in range(3):
                        push = weight * d[c]
                        acc[t][c] = push if acc[t][c] is None else acc[t][c] + push
                        pushed[c] = push if pushed[c] is None else pushed[c] + push
                for c in range(3):
                    fj[c * slots + b] = fj[c * slots + b] + pushed[c]
            for t in range(group):
                for c in range(3):
                    acc_ref[c * slots + a, at[t], :] = acc[t][c]
        return carry

    lax.fori_loop(0, LANES // (8 * group), block, 0)
    for c in range(3):
        for a in range(slots):
            k = c * slots + a
            total = -jnp.sum(fj[k], axis=0, keepdims=True)
            if a < slots - 2:
                total = total + jnp.sum(acc_ref[k].T, axis=0, keepdims=True)
            force[c, a:a + 1, :] = GAIN * total
    for store in stores:
        store.wait()


def body(
    slabs, gores,
    fluid_velocity, viscosity, pressure_jump, normals, canopy_position, tension,
    slot_cut, couple_dest, couple_block, contact_owner, contact_row,
):
    cz, cy, nx = viscosity.shape
    rows = pressure_jump.shape[0]
    devices = slabs * gores
    zy = cz * cy
    nbx = nx // LANES
    vmem = pl.BlockSpec(memory_space=pltpu.VMEM)
    anywhere = pl.BlockSpec(memory_space=pl.ANY)
    dma = pltpu.SemaphoreType.DMA
    cut_width = min(LANES, slot_cut.shape[0])
    tall = rows + 2 * HALO
    fluid, canopy, sets = pl.pallas_call(
        functools.partial(main_kernel, slabs, gores),
        out_shape=(
            jax.ShapeDtypeStruct(fluid_velocity.shape, F32),
            jax.ShapeDtypeStruct(canopy_position.shape, F32),
            jax.ShapeDtypeStruct((gores * 8, LANES), F32),
        ),
        in_specs=[pl.BlockSpec(memory_space=pltpu.HBM)] * 11,
        out_specs=(vmem, vmem, vmem),
        scratch_shapes=[
            pltpu.VMEM(pressure_jump.shape, F32),
            pltpu.VMEM(normals.shape, F32),
            pltpu.VMEM(canopy_position.shape, F32),
            pltpu.VMEM(tension.shape, F32),
            pltpu.VMEM((slot_cut.shape[0] // cut_width, cut_width), jnp.int32),
            pltpu.VMEM((2, rows), jnp.int32),
            pltpu.VMEM((2, rows), jnp.int32),
            pltpu.VMEM(contact_row.shape, jnp.int32),
            pltpu.VMEM(contact_row.shape, jnp.int32),
            pltpu.VMEM((STEPS, 3, cz + 2, cy, nx), F32),
            pltpu.VMEM((cz, cy, nx), F32),
            pltpu.VMEM((STEPS, 2, 3, cz, nx), F32),
            pltpu.VMEM((STEPS, 2, 3, cz, nx), F32),
            pltpu.VMEM((devices * 8, LANES), F32),
            pltpu.VMEM((devices * 8, LANES), F32),
            pltpu.VMEM((devices * 8, LANES), F32),
            pltpu.VMEM((devices * 8, LANES), F32),
            pltpu.VMEM((nbx, zy - 2 * (zy // cz), 2 * devices), BF16),
            pltpu.VMEM((nbx, 2 * devices, zy), BF16),
            pltpu.VMEM((7, tall, LANES), F32),
            pltpu.VMEM((rows, LANES), F32),
            pltpu.VMEM((rows, LANES), F32),
            pltpu.VMEM((tall, LANES), F32),
            pltpu.VMEM((tall, LANES), F32),
            pltpu.VMEM((3, tall, LANES), F32),
            pltpu.VMEM((rows, LANES), F32),
            pltpu.VMEM((rows, LANES), F32),
            pltpu.VMEM((tall, LANES), F32),
            pltpu.VMEM((tall, LANES), F32),
            pltpu.VMEM((10, tall, 2 * LANES), F32),
            pltpu.VMEM((rows, LANES), F32),
            pltpu.VMEM((gores * 8, LANES), F32),
            pltpu.VMEM((gores * 8, LANES), F32),
            dma((9,)),
            dma((4,)),
            dma((STEPS, 2, 3)),
            dma((STEPS, 2, 3)),
            dma((STEPS, 2, 3)),
            dma((STEPS, 2, 3)),
            dma((4,)),
            dma((16,)),
            dma((16,)),
            dma((2,)),
        ],
        compiler_params=pltpu.CompilerParams(
            collective_id=0, has_side_effects=True, vmem_limit_bytes=26 << 20
        ),
        name="fluid_membrane",
    )(*(
        pltpu.with_memory_space_constraint(x, pltpu.HBM)
        for x in (
            fluid_velocity, viscosity, pressure_jump, normals, canopy_position, tension,
            slot_cut.reshape(-1, cut_width),
            couple_dest[0].T, couple_block[0].T, contact_owner[:, :, 0], contact_row,
        )
    ))
    slots = 2 * gores
    fluid, canopy, force = pl.pallas_call(
        functools.partial(contact_kernel, gores),
        out_shape=(
            jax.ShapeDtypeStruct(fluid.shape, F32),
            jax.ShapeDtypeStruct(canopy.shape, F32),
            jax.ShapeDtypeStruct((3, slots, LANES), F32),
        ),
        in_specs=[vmem, vmem, vmem],
        out_specs=(anywhere, anywhere, vmem),
        scratch_shapes=[
            pltpu.VMEM((3 * slots, 8, LANES), F32),
            pltpu.VMEM((3 * slots, 8, LANES), F32),
            pltpu.VMEM((3 * slots, LANES, LANES), F32),
            pltpu.VMEM((LANES, LANES), F32),
            dma((2,)),
        ],
        compiler_params=pltpu.CompilerParams(vmem_limit_bytes=28 << 20),
        name="contact",
    )(fluid, canopy, sets)
    return fluid, canopy, jnp.swapaxes(force, 0, 1)[None, None]


def solution(mesh):
    in_specs = (
        P(None, "slab", "gore", None),
        P("slab", "gore", None),
        P("slab", "gore"),
        P(None, "slab", "gore"),
        P(None, "slab", "gore"),
        P(None, "slab", "gore"),
        P(),
        P("gore", "slab", None),
        P("gore", "slab", None),
        P("gore", "slab", None),
        P("gore", "slab"),
    )
    out_specs = (
        P(None, "slab", "gore", None),
        P(None, "slab", "gore"),
        P("slab", "gore", None, None, None),
    )
    step = functools.partial(body, mesh.shape["slab"], mesh.shape["gore"])
    return jax.shard_map(step, mesh=mesh, in_specs=in_specs, out_specs=out_specs, check_vma=False)
```
